256 devices in a mesh: row: 8 (over y, core), col: 32 (over z, x).
Axes of the slice: x: 4, y: 4, z: 8, core: 2. Of those that a mesh axis runs over, the one named last changes fastest.
Arguments:
- hidden: bfloat16 [1024, 24576], P(None, 'row'), may hold values from -6 to 6
- down_weight: bfloat16 [24576, 6144], P('row', 'col'), may hold values from -0.0390625 to 0.0390625
- residual: bfloat16 [1024, 6144], P('row', 'col'), may hold values from -260 to 260
- gain: bfloat16 [6144], P('col'), may hold values from 0.099609375 to 1.8984375
- qk_weight: bfloat16 [6144, 12288], P(None, 'col'), may hold values from -0.078125 to 0.078125
Outputs:
- stream: bfloat16 [1024, 6144], P('row', 'col')
- queries_keys: bfloat16 [1024, 12288], P('row', 'col')
The draws below stay inside these ranges and needn't reach their ends.
All inputs are finite; a program needn't handle non-finite values.
Results may differ from the reference program's by a relative error of at most 0.015.
Values may be sent and summed in bfloat16 or wider, within the bound.
A program may use at most 64 MiB of HBM per device.

```python
import jax
import jax.numpy as jnp
from jax import lax

D = 6144
FF = 24576
TOKENS = 1024


def draw_residual(key, part):
    key_col = jax.random.fold_in(key, 11)
    key_row = jax.random.fold_in(key, 12)
    key_val = jax.random.fold_in(key, 13)
    across = jnp.arange(D, dtype=jnp.float32) / jnp.float32(max(D - 1, 1))
    col_scale = jnp.exp(across * jnp.log(3.0)) * jax.random.uniform(key_col, (D,), jnp.float32, 0.7, 1.4)
    row_scale = jnp.exp(jax.random.uniform(key_row, (TOKENS, 1), jnp.float32, 0.0, 1.0) * jnp.log(10.0))
    base = jnp.clip(jax.random.normal(key_val, (TOKENS, D), jnp.float32), -6.0, 6.0)
    values = base * row_scale * col_scale[None, :]
    return values.astype(jnp.bfloat16)


def raised(array, stream_key, source, target, blocks, factor):
    def block_of(dim):
        return (jnp.arange(array.shape[dim]) // (array.shape[dim] // blocks)).reshape((-1,) + (1,) * (array.ndim - 1 - dim))

    one_side = jax.random.permutation(stream_key, blocks)[block_of(target)]
    second = (block_of(target) + blocks // 2) % blocks
    return jnp.where((block_of(source) == one_side) | (block_of(source) == second), factor * array, array)


def block_scale(stream_key, shape, pieces, smallest, largest):
    def one(dim, parts):
        steps = jax.random.uniform(jax.random.fold_in(jax.random.fold_in(stream_key, 6), dim), (parts,), jnp.float32, smallest / len(pieces), largest / len(pieces))
        return jnp.repeat(jnp.exp(steps), shape[dim] // parts).reshape((-1,) + (1,) * (len(shape) - dim - 1))

    loudness = one(*pieces[0])
    for cut in pieces[1:]:
        loudness = loudness * one(*cut)
    return loudness


def bell_draw(stream_key, shape, scale, reach, shards=(), held_as=jnp.bfloat16):
    level = block_scale(stream_key, shape, shards, -0.22, 0.18) if shards else 1.0
    drawn = jax.random.normal(stream_key, shape, jnp.float32) * scale * level
    return jnp.minimum(jnp.maximum(drawn, -reach), reach).astype(held_as)


def gaussian_with(own_key, shape, spread, limit, cuts, heavy, kind=jnp.bfloat16):
    entries = spread * jax.random.normal(own_key, shape, jnp.float32)
    if cuts:
        entries = entries * block_scale(own_key, shape, cuts, -0.22, 0.18)
    return jnp.clip(raised(entries, jax.random.fold_in(own_key, 3), *heavy), -limit, limit).astype(kind)


def setup_inputs(seed: int = 0) -> dict:
    streams_of = jax.random.split(jax.random.key(seed), 6)
    return {
        "hidden": gaussian_with(streams_of[0], (TOKENS, FF), 1.0, 6.0, ((1, 8),), (1, 0, 8, 2.0)),
        "down_weight": bell_draw(streams_of[1], (FF, D), FF ** -0.5, 0.0390625, ((0, 8), (1, 32))),
        "residual": draw_residual(jax.random.fold_in(streams_of[5], 71), 0),
        "gain": jnp.clip(1.0 + 0.18 * jax.random.normal(streams_of[3], (D,), jnp.float32), 0.099609375, 1.8984375).astype(jnp.bfloat16),
        "qk_weight": bell_draw(streams_of[4], (D, 2 * D), D ** -0.5, 0.078125, ((1, 32),)),
    }


def reference(hidden, down_weight, residual, gain, qk_weight):
    mlp = jnp.dot(hidden, down_weight, preferred_element_type=jnp.float32)
    stream = (residual.astype(jnp.float32) + mlp).astype(jnp.bfloat16)
    values = stream.astype(jnp.float32)
    mean = lax.optimization_barrier(jnp.mean(values, axis=1, keepdims=True))
    var = lax.optimization_barrier(jnp.mean((values - mean) * (values - mean), axis=1, keepdims=True))
    normed = ((values - mean) / jnp.sqrt(var + 1e-06) * gain.astype(jnp.float32)[None, :]).astype(jnp.bfloat16)
    queries_keys = jnp.dot(normed, qk_weight, preferred_element_type=jnp.float32).astype(jnp.bfloat16)
    return (stream, queries_keys)
```

```python
import functools

import jax
import jax.numpy as jnp
from jax import lax
from jax.experimental import pallas as pl
from jax.experimental.pallas import tpu as pltpu
from jax.sharding import PartitionSpec as P

MESH = pl.DeviceIdType.MESH
F32, BF16 = jnp.float32, jnp.bfloat16
NX, NZ, NY = 4, 8, 4
ROWS, COLS = 2 * NY, NZ * NX
TOK, WIDE = 128, 128
NARROW = 64


def lanes(shape):
    return lax.broadcasted_iota(jnp.int32, shape, len(shape) - 1)


def kernel(
    hidden, down, residual, gain, weight, stream_out, qk_out,
    hid_v, down_a, down_n, down_b, res_v, gain_in, gains, w_v, stream_v, qk_v,
    rs_send, rs_recv, ga, gb,
    load_sem, rs_ssem, rs_rsem, gx_ssem, gx_rsem, gz_ssem, gz_rsem,
    a_rsem, a4_rsem, bx_rsem, bz_rsem, bz4_rsem, ag_ssem, out_sem,
):
    row, col = lax.axis_index("row"), lax.axis_index("col")
    y, core = row // 2, row % 2
    z, x = col // NX, col % NX

    def at(zz, xx):
        return (row, zz * NX + xx)

    def zs(d):
        return lax.rem(z + d + NZ, NZ)

    def xs(d):
        return lax.rem(x + d + NX, NX)

    def load(src, dst, sem):
        copy = pltpu.make_async_copy(src, dst, load_sem.at[sem])
        copy.start()
        return copy

    c_down_a = load(down.at[:, pl.ds(0, WIDE)], down_a, 0)
    c_down_n = load(down.at[:, pl.ds(WIDE, NARROW)], down_n, 1)
    c_hid = []
    order = (2, 1, 3, 0)
    for i, d in enumerate(order):
        rows = pl.ds(pl.multiple_of(lax.rem(y + d, NY) * 2 * TOK, 2 * TOK), 2 * TOK)
        c_hid.append(load(hidden.at[rows], hid_v.at[i], 2 + i))
    c_gain = load(gain, gain_in, 6)
    c_res = load(residual, res_v, 7)
    c_w = load(weight, w_v, 8)

    barrier = pltpu.get_barrier_semaphore()
    peers = [(lax.rem(row + d, ROWS), col) for d in range(1, ROWS)]
    peers += [at(z, xs(d)) for d in range(1, NX)]
    peers += [at(zs(d), x) for d in range(1, NZ)]
    for peer in peers:
        pl.semaphore_signal(barrier, inc=1, device_id=peer, device_id_type=MESH)

    c_gain.wait()
    g = gain_in[...].astype(F32)
    gn = g[:, WIDE:]
    gains[col] = jnp.concatenate([g[:, :WIDE], gn, gn], axis=1)
    pl.semaphore_wait(barrier, len(peers))

    def send(src, dst, ssem, rsem, peer):
        copy = pltpu.make_async_remote_copy(
            src_ref=src, dst_ref=dst, send_sem=ssem, recv_sem=rsem,
            device_id=peer, device_id_type=MESH,
        )
        copy.start()
        return copy

    def arrived(ref, rsem):
        pltpu.make_async_copy(ref, ref, rsem).wait()

    sends = []
    for d in range(1, NX):
        sends.append(send(gains.at[col], gains.at[col], gx_ssem.at[d - 1], gx_rsem.at[NX - 1 - d], at(z, xs(d))))

    c_down_n.wait()
    n = down_n[...]
    down_b[...] = jnp.concatenate([n, n], axis=1)
    c_down_a.wait()
    lane = lanes((NARROW, WIDE))
    own_a = own_b = None
    for i, d in enumerate(order):
        c_hid[i].wait()
        h = hid_v[i]
        pa = jnp.dot(h, down_a[...], preferred_element_type=F32)
        pb = jnp.dot(h, down_b[...], preferred_element_type=F32)
        yy = lax.rem(y + d, NY)
        for k in range(2):
            a = pa[k * TOK:(k + 1) * TOK]
            b = pb[k * TOK:(k + 1) * TOK]
            b = jnp.where(lane < NARROW, b[:NARROW], b[NARROW:])
            rs_send[2 * i + k, :TOK] = a.astype(BF16)
            rs_send[2 * i + k, TOK:] = b.astype(BF16)
        for k in range(2):
            peer = (yy * 2 + k, col)
            if d:
                sends.append(send(rs_send.at[2 * i + k], rs_recv.at[row], rs_ssem.at[2 * i + k], rs_rsem.at[row], peer))
            else:
                @pl.when(core != k)
                def _():
                    send(rs_send.at[2 * i + k], rs_recv.at[row], rs_ssem.at[2 * i + k], rs_rsem.at[row], peer)

                @pl.when(core == k)
                def _():
                    rs_recv[row] = rs_send[2 * i + k]

    for d in range(NX - 1):
        slot = z * NX + lax.rem(x + d + 1, NX)
        arrived(gains.at[slot], gx_rsem.at[d])
    four = gains.at[pl.ds(z * NX, NX)]
    for d in range(1, NZ):
        sends.append(send(four, four, gz_ssem.at[d - 1], gz_rsem.at[NZ - 1 - d], at(zs(d), x)))

    for d in range(1, ROWS):
        r = lax.rem(row + d, ROWS)
        arrived(rs_recv.at[r], rs_rsem.at[r])
    c_res.wait()
    res = res_v[...].astype(F32)
    total = jnp.zeros((TOK + NARROW, WIDE), F32)
    for r in range(ROWS):
        total = total + rs_recv[r].astype(F32)
    sa = (res[:, :WIDE] + total[:TOK]).astype(BF16)
    rb = jnp.concatenate([res[:NARROW, WIDE:], res[NARROW:, WIDE:]], axis=1)
    sb32 = rb + total[TOK:]
    sb = sb32.astype(BF16)
    ga[col] = sa
    gb[col] = sb

    nag = [0]

    def push(src, rsem, peer):
        sends.append(send(src, src, ag_ssem.at[nag[0]], rsem, peer))
        nag[0] += 1

    def slot_a(dz, dx):
        return zs(dz) * NX + xs(dx)

    half = pl.ds(0, TOK // 2), pl.ds(TOK // 2, TOK // 2)
    bhalf = pl.ds(0, NARROW // 2), pl.ds(NARROW // 2, NARROW // 2)

    push(gb.at[col], bx_rsem.at[0], at(z, xs(1)))
    push(gb.at[col], bx_rsem.at[1], at(z, xs(-1)))
    push(ga.at[col], a_rsem.at[col], at(zs(1), x))
    push(ga.at[col], a_rsem.at[col], at(zs(-1), x))
    push(ga.at[col], a_rsem.at[col], at(z, xs(1)))
    push(ga.at[col], a_rsem.at[col], at(z, xs(-1)))

    stream_v[:, :WIDE] = sa
    back = sb32.astype(BF16)
    stream_v[:NARROW, WIDE:] = back[:, :NARROW]
    stream_v[NARROW:, WIDE:] = back[:, NARROW:]
    c_stream = pltpu.make_async_copy(stream_v, stream_out, out_sem.at[0])
    c_stream.start()

    def a_from_z(d):
        if d < 4:
            for s in (-1, 1):
                slot = slot_a(s * d, 0)
                arrived(ga.at[slot], a_rsem.at[slot])
                if d < 3:
                    push(ga.at[slot], a_rsem.at[slot], at(zs(-s), x))
                else:
                    h = half[0] if s < 0 else half[1]
                    push(ga.at[slot, h], a4_rsem.at[0 if s < 0 else 1], at(zs(-s), x))
                push(ga.at[slot], a_rsem.at[slot], at(z, xs(1)))
                push(ga.at[slot], a_rsem.at[slot], at(z, xs(-1)))
        else:
            slot = slot_a(4, 0)
            for k in range(2):
                arrived(ga.at[slot, half[k]], a4_rsem.at[k])
            push(ga.at[slot], a_rsem.at[slot], at(z, xs(1)))
            push(ga.at[slot], a_rsem.at[slot], at(z, xs(-1)))

    def a_from_x(dz):
        for s in (-1, 1):
            slot = slot_a(dz, s)
            arrived(ga.at[slot], a_rsem.at[slot])
            h = half[0] if s < 0 else half[1]
            push(ga.at[slot, h], ax2_rsem(dz, 0 if s < 0 else 1), at(z, xs(-s)))

    def ax2_rsem(dz, k):
        return ax2.at[zs(dz), k]

    ax2 = bz4_rsem.at[pl.ds(1, NZ)]

    def a_relayed(dz):
        slot = slot_a(dz, 2)
        for k in range(2):
            arrived(ga.at[slot, half[k]], ax2_rsem(dz, k))

    def b_of(dz):
        return gb.at[pl.ds(zs(dz) * NX, NX)]

    def b_from_z(d):
        if d < 4:
            for s in (-1, 1):
                arrived(b_of(s * d), bz_rsem.at[zs(s * d)])
                if d < 3:
                    push(b_of(s * d), bz_rsem.at[zs(s * d)], at(zs(-s), x))
                else:
                    k = 0 if s < 0 else 1
                    part = gb.at[pl.ds(zs(s * d) * NX + 2 * k, 2)]
                    push(part, bz4_rsem.at[0, k], at(zs(-s), x))
        else:
            for k in range(2):
                part = gb.at[pl.ds(zs(4) * NX + 2 * k, 2)]
                arrived(part, bz4_rsem.at[0, k])

    left, right = z * NX + xs(-1), z * NX + xs(1)
    arrived(gb.at[left], bx_rsem.at[0])
    push(gb.at[left, bhalf[0]], bx_rsem.at[2], at(z, xs(1)))
    arrived(gb.at[right], bx_rsem.at[1])
    push(gb.at[right, bhalf[1]], bx_rsem.at[3], at(z, xs(-1)))
    a_from_z(1)
    a_from_x(0)
    far = z * NX + xs(2)
    arrived(gb.at[far, bhalf[0]], bx_rsem.at[2])
    arrived(gb.at[far, bhalf[1]], bx_rsem.at[3])
    push(b_of(0), bz_rsem.at[z], at(zs(1), x))
    push(b_of(0), bz_rsem.at[z], at(zs(-1), x))
    a_from_z(2)
    a_from_x(1)
    a_from_x(-1)
    b_from_z(1)
    a_from_z(3)
    a_from_x(2)
    a_from_x(-2)
    b_from_z(2)
    a_from_z(4)
    a_from_x(3)
    a_from_x(-3)
    b_from_z(3)
    a_from_x(4)
    for dz in range(NZ):
        a_relayed(dz)
    b_from_z(4)

    for d in range(NZ - 1):
        arrived(gains.at[pl.ds(zs(d + 1) * NX, NX)], gz_rsem.at[d])
    c_w.wait()

    inv = 1.0 / (COLS * (WIDE + NARROW))

    def total_step(c, carry):
        ta, tb = carry
        return ta + ga[c].astype(F32), tb + gb[c].astype(F32)

    zero = jnp.zeros((TOK, WIDE), F32), jnp.zeros((NARROW, WIDE), F32)

    def rows_of(ta, tb):
        low = jnp.sum(jnp.where(lane < NARROW, tb, 0.0), axis=1, keepdims=True)
        high = jnp.sum(jnp.where(lane < NARROW, 0.0, tb), axis=1, keepdims=True)
        return jnp.sum(ta, axis=1, keepdims=True) + jnp.concatenate([low, high], axis=0)

    def spread(v):
        wide = jnp.broadcast_to(v, (TOK, WIDE))
        return wide, jnp.where(lane < NARROW, wide[:NARROW], wide[NARROW:])

    mean = rows_of(*lax.fori_loop(0, COLS, total_step, zero)) * inv
    mean_a, mean_b = spread(mean)

    def var_step(c, carry):
        ta, tb = carry
        da, db = ga[c].astype(F32) - mean_a, gb[c].astype(F32) - mean_b
        return ta + da * da, tb + db * db

    var = rows_of(*lax.fori_loop(0, COLS, var_step, zero)) * inv
    rstd_a, rstd_b = spread(1.0 / jnp.sqrt(var + 1e-6))

    qk_v[...] = jnp.zeros_like(qk_v)

    @pl.loop(0, COLS // 2)
    def _(p):
        def normed(c):
            gg = gains[c]
            na = (ga[c].astype(F32) - mean_a) * rstd_a * gg[:, :WIDE]
            nb = (gb[c].astype(F32) - mean_b) * rstd_b * gg[:, WIDE:]
            return na.astype(BF16), nb

        a0, b0 = normed(2 * p)
        a1, b1 = normed(2 * p + 1)
        top = jnp.where(lane < NARROW, b0, pltpu.roll(b1, NARROW, 1))
        bottom = jnp.where(lane < NARROW, pltpu.roll(b0, NARROW, 1), b1)
        bb = jnp.concatenate([top, bottom], axis=0).astype(BF16)
        lhs = jnp.concatenate([a0, a1, bb], axis=1)
        w = w_v[p]
        rhs = jnp.concatenate([w[:128], w[192:320], w[128:192], w[320:384]], axis=0)
        qk_v[...] += jnp.dot(lhs, rhs, preferred_element_type=F32)

    qk_b = hid_v.at[0, pl.ds(0, TOK), pl.ds(0, qk_v.shape[1])]
    qk_b[...] = qk_v[...].astype(BF16)
    c_qk = pltpu.make_async_copy(qk_b, qk_out, out_sem.at[1])
    c_qk.start()
    for copy in sends:
        copy.wait_send()
    for k in range(2):
        @pl.when(core != k)
        def _():
            pltpu.make_async_copy(rs_send.at[6 + k], rs_send.at[6 + k], rs_ssem.at[6 + k]).wait()
    c_stream.wait()
    c_qk.wait()


def per_device(hidden, down_weight, residual, gain, qk_weight):
    depth, width = down_weight.shape
    full, heads = qk_weight.shape
    any_spec = pl.BlockSpec(memory_space=pl.ANY)
    dma = pltpu.SemaphoreType.DMA
    return pl.pallas_call(
        kernel,
        out_shape=(
            jax.ShapeDtypeStruct((TOK, width), BF16),
            jax.ShapeDtypeStruct((TOK, heads), BF16),
        ),
        in_specs=[any_spec] * 5,
        out_specs=(any_spec, any_spec),
        scratch_shapes=[
            pltpu.VMEM((NY, 2 * TOK, depth), BF16),
            pltpu.VMEM((depth, WIDE), BF16),
            pltpu.VMEM((depth, NARROW), BF16),
            pltpu.VMEM((depth, WIDE), BF16),
            pltpu.VMEM((TOK, width), BF16),
            pltpu.VMEM((1, width), BF16),
            pltpu.VMEM((COLS, 1, WIDE + 2 * NARROW), F32),
            pltpu.VMEM((COLS // 2, 2 * width, heads), BF16),
            pltpu.VMEM((TOK, width), BF16),
            pltpu.VMEM((TOK, heads), F32),
            pltpu.VMEM((ROWS, TOK + NARROW, WIDE), BF16),
            pltpu.VMEM((ROWS, TOK + NARROW, WIDE), BF16),
            pltpu.VMEM((COLS, TOK, WIDE), BF16),
            pltpu.VMEM((COLS, NARROW, WIDE), BF16),
            dma((9,)),
            dma((ROWS,)), dma((ROWS,)),
            dma((NX - 1,)), dma((NX - 1,)),
            dma((NZ - 1,)), dma((NZ - 1,)),
            dma((COLS,)), dma((2,)), dma((4,)), dma((NZ,)), dma((NZ + 1, 2)),
            dma((72,)), dma((2,)),
        ],
        compiler_params=pltpu.CompilerParams(
            collective_id=0, has_side_effects=True, vmem_limit_bytes=56 * 1024 * 1024
        ),
    )(hidden, down_weight, residual, gain.reshape(1, width), qk_weight.reshape(COLS // 2, 2 * width, heads))


def solution(mesh):
    placed = (P(None, "row"), P("row", "col"), P("row", "col"), P("col"), P(None, "col"))
    return jax.shard_map(
        per_device,
        mesh=mesh,
        in_specs=placed,
        out_specs=(P("row", "col"), P("row", "col")),
        check_vma=False,
    )
```

```python
import functools

import jax
import jax.numpy as jnp
from jax import lax
from jax.experimental import pallas as pl
from jax.experimental.pallas import tpu as pltpu
from jax.sharding import PartitionSpec as P

MESH = pl.DeviceIdType.MESH
F32, BF16 = jnp.float32, jnp.bfloat16
NX, NZ, NY = 4, 8, 4
ROWS, COLS = 2 * NY, NZ * NX
TOK = 128
X_FIRST = 48
STEPS_Z = (1, -1, 2, -2, 3, -3, 4)
STEPS_X = (1, -1, 2)


def merge(stats, count):
    means, squares = stats[:, 0], stats[:, 1]
    mean = jnp.mean(means, axis=0, keepdims=True)
    off = means - mean
    square = jnp.sum(squares, axis=0, keepdims=True) + count * jnp.sum(off * off, axis=0, keepdims=True)
    return jnp.concatenate([mean, square], axis=0)


def kernel(
    hidden, down, residual, gain, weight, stream_out, qk_out,
    hid_v, down_v, res_v, gain_in, gains, gain_rows, w_v, qk_v, qk_b,
    rs_send, rs_recv, g, stats_z, stats_x,
    load_sem, rs_ssem, rs_rsem, gx_ssem, gx_rsem, gz_ssem, gz_rsem,
    sx_ssem, sx_rsem, sz_ssem, sz_rsem,
    a_rsem, bx_rsem, bz_rsem, ag_ssem, out_sem,
):
    row, col = lax.axis_index("row"), lax.axis_index("col")
    y, core = row // 2, row % 2
    z, x = col // NX, col % NX
    wide = down.shape[0]

    def at(zz, xx):
        return (row, zz * NX + xx)

    def zs(d):
        return lax.rem(z + d + NZ, NZ)

    def xs(d):
        return lax.rem(x + d + NX, NX)

    def load(src, dst, sem):
        copy = pltpu.make_async_copy(src, dst, load_sem.at[sem])
        copy.start()
        return copy

    c_gain = load(gain, gain_in, 6)
    c_down = load(down, down_v, 0)
    c_hid = []
    order = (2, 1, 3, 0)
    for i, d in enumerate(order):
        rows = pl.ds(pl.multiple_of(lax.rem(y + d, NY) * 2 * TOK, 2 * TOK), 2 * TOK)
        c_hid.append(load(hidden.at[rows], hid_v.at[i], 2 + i))
    c_res = load(residual, res_v, 7)

    barrier = pltpu.get_barrier_semaphore()
    peers = [(lax.rem(row + d, ROWS), col) for d in range(1, ROWS)]
    peers += [at(z, xs(d)) for d in STEPS_X]
    peers += [at(zs(d), x) for d in STEPS_Z]
    for peer in peers:
        pl.semaphore_signal(barrier, inc=1, device_id=peer, device_id_type=MESH)

    c_gain.wait()
    gains[col] = gain_in[...].astype(F32)
    pl.semaphore_wait(barrier, len(peers))

    sends = []

    def send(src, dst, ssem, rsem, peer):
        copy = pltpu.make_async_remote_copy(
            src_ref=src, dst_ref=dst, send_sem=ssem, recv_sem=rsem,
            device_id=peer, device_id_type=MESH,
        )
        copy.start()
        return copy

    def arrived(ref, rsem):
        pltpu.make_async_copy(ref, ref, rsem).wait()

    def over_x(ref, ssem, rsem):
        for i, d in enumerate(STEPS_X):
            sends.append(send(ref, ref, ssem.at[i], rsem.at[x], at(z, xs(d))))

    def over_z(ref, ssem, rsem):
        for i, d in enumerate(STEPS_Z):
            sends.append(send(ref, ref, ssem.at[i], rsem.at[z], at(zs(d), x)))

    over_x(gains.at[col], gx_ssem, gx_rsem)

    c_down.wait()
    for i, d in enumerate(order):
        c_hid[i].wait()
        part = lax.dot_general(
            down_v[...], hid_v[i], (((1,), (1,)), ((), ())), preferred_element_type=F32
        ).astype(BF16)
        yy = lax.rem(y + d, NY)
        for k in range(2):
            rs_send[2 * i + k] = part[:, k * TOK:(k + 1) * TOK]
        for k in range(2):
            peer = (yy * 2 + k, col)
            if d:
                sends.append(send(rs_send.at[2 * i + k], rs_recv.at[row], rs_ssem.at[2 * i + k], rs_rsem.at[row], peer))
            else:
                @pl.when(core != k)
                def _():
                    send(rs_send.at[2 * i + k], rs_recv.at[row], rs_ssem.at[2 * i + k], rs_rsem.at[row], peer)

                @pl.when(core == k)
                def _():
                    rs_recv[row] = rs_send[2 * i + k]

    c_w = load(weight, w_v, 8)

    for d in STEPS_X:
        arrived(gains.at[z * NX + xs(d)], gx_rsem.at[xs(d)])
    over_z(gains.at[pl.ds(z * NX, NX)], gz_ssem, gz_rsem)

    for d in range(1, ROWS):
        r = lax.rem(row + d, ROWS)
        arrived(rs_recv.at[r], rs_rsem.at[r])
    c_res.wait()
    total = rs_recv[0].astype(F32)
    for r in range(1, ROWS):
        total = total + rs_recv[r].astype(F32)
    stream = (res_v[...].astype(F32) + total).astype(BF16)
    g[col] = stream

    last = pl.ds(X_FIRST, wide - X_FIRST)
    first = pl.ds(0, X_FIRST)
    count = [0]

    def push(ref, rsem, peer):
        sends.append(send(ref, ref, ag_ssem.at[count[0]], rsem, peer))
        count[0] += 1

    def push_x(dz):
        slot = zs(dz) * NX + x
        for e in STEPS_X:
            push(g.at[slot, last], a_rsem.at[slot], at(z, xs(e)))

    def group(dz):
        return g.at[pl.ds(zs(dz) * NX, NX), first]

    for e in STEPS_X:
        push(g.at[col, first], bx_rsem.at[x], at(z, xs(e)))
    for d in STEPS_Z:
        push(g.at[col, last], a_rsem.at[col], at(zs(d), x))

    values = stream.astype(F32)
    mean = jnp.mean(values, axis=0, keepdims=True)
    off = values - mean
    stats_z[z] = jnp.concatenate([mean, jnp.sum(off * off, axis=0, keepdims=True)], axis=0)
    over_z(stats_z.at[z], sz_ssem, sz_rsem)
    push_x(0)
    c_stream = pltpu.make_async_copy(g.at[col], stream_out, out_sem.at[0])
    c_stream.start()

    for e in STEPS_X:
        arrived(g.at[z * NX + xs(e), first], bx_rsem.at[xs(e)])
    for d in (4, 3, -3, 2, -2, 1, -1):
        push(group(0), bz_rsem.at[z], at(zs(d), x))

    for d in STEPS_Z:
        arrived(gains.at[pl.ds(zs(d) * NX, NX)], gz_rsem.at[zs(d)])
    for c in range(NZ):
        gain_rows[c] = jnp.concatenate([gains[c * NX + k] for k in range(NX)], axis=1)

    def from_z(d):
        slot = zs(d) * NX + x
        arrived(g.at[slot, last], a_rsem.at[slot])
        push_x(d)

    for d in STEPS_Z[:4]:
        from_z(d)
    for d in STEPS_Z:
        arrived(stats_z.at[zs(d)], sz_rsem.at[zs(d)])
    stats_x[x] = merge(stats_z[...], wide)
    over_x(stats_x.at[x], sx_ssem, sx_rsem)
    for d in STEPS_Z[4:]:
        from_z(d)

    for e in STEPS_X:
        arrived(stats_x.at[xs(e)], sx_rsem.at[xs(e)])
    both = merge(stats_x[...], NZ * wide)
    scale = 1.0 / jnp.sqrt(both[1:] * (1.0 / (COLS * wide)) + 1e-6)
    mean_t = jnp.transpose(jnp.broadcast_to(both[:1], (TOK, TOK)))
    scale_t = jnp.transpose(jnp.broadcast_to(scale, (TOK, TOK)))
    c_w.wait()

    for i, d in enumerate((0,) + STEPS_Z):
        for e in STEPS_X:
            slot = zs(d) * NX + xs(e)
            arrived(g.at[slot, last], a_rsem.at[slot])
        if d:
            arrived(group(d), bz_rsem.at[zs(d)])
        zz = zs(d)
        block = g[pl.ds(zz * NX, NX)].reshape(NX * wide, TOK)
        tokens = jnp.transpose(block)
        row_gain = gain_rows[zz]
        pieces = []
        for k in range(NX * wide // TOK):
            lanes = slice(k * TOK, (k + 1) * TOK)
            piece = (tokens[:, lanes].astype(F32) - mean_t) * scale_t * row_gain[:, lanes]
            pieces.append(piece.astype(BF16))
        out = jnp.dot(jnp.concatenate(pieces, axis=1), w_v[zz], preferred_element_type=F32)
        if i == 0:
            qk_v[...] = out
        elif i < NZ - 1:
            qk_v[...] += out
        else:
            qk_b[...] = (qk_v[...] + out).astype(BF16)

    c_qk = pltpu.make_async_copy(qk_b, qk_out, out_sem.at[1])
    c_qk.start()
    for copy in sends:
        copy.wait_send()
    for k in range(2):
        @pl.when(core != k)
        def _():
            pltpu.make_async_copy(rs_send.at[6 + k], rs_send.at[6 + k], rs_ssem.at[6 + k]).wait()
    c_stream.wait()
    c_qk.wait()


def per_device(hidden, down_weight, residual, gain, qk_weight):
    depth, width = down_weight.shape
    full, heads = qk_weight.shape
    any_spec = pl.BlockSpec(memory_space=pl.ANY)
    dma = pltpu.SemaphoreType.DMA
    stream, queries_keys = pl.pallas_call(
        kernel,
        out_shape=(
            jax.ShapeDtypeStruct((width, TOK), BF16),
            jax.ShapeDtypeStruct((TOK, heads), BF16),
        ),
        in_specs=[any_spec] * 5,
        out_specs=(any_spec, any_spec),
        scratch_shapes=[
            pltpu.VMEM((NY, 2 * TOK, depth), BF16),
            pltpu.VMEM((width, depth), BF16),
            pltpu.VMEM((width, TOK), BF16),
            pltpu.VMEM((1, width), BF16),
            pltpu.VMEM((COLS, 1, width), F32),
            pltpu.VMEM((NZ, 1, NX * width), F32),
            pltpu.VMEM((NZ, NX * width, heads), BF16),
            pltpu.VMEM((TOK, heads), F32),
            pltpu.VMEM((TOK, heads), BF16),
            pltpu.VMEM((ROWS, width, TOK), BF16),
            pltpu.VMEM((ROWS, width, TOK), BF16),
            pltpu.VMEM((COLS, width, TOK), BF16),
            pltpu.VMEM((NZ, 2, TOK), F32),
            pltpu.VMEM((NX, 2, TOK), F32),
            dma((9,)),
            dma((ROWS,)), dma((ROWS,)),
            dma((NX - 1,)), dma((NX,)), dma((NZ - 1,)), dma((NZ,)),
            dma((NX - 1,)), dma((NX,)), dma((NZ - 1,)), dma((NZ,)),
            dma((COLS,)), dma((NX,)), dma((NZ,)),
            dma((48,)), dma((2,)),
        ],
        compiler_params=pltpu.CompilerParams(
            collective_id=0, has_side_effects=True, vmem_limit_bytes=56 * 1024 * 1024
        ),
    )(
        hidden, down_weight.T, residual.T, gain.reshape(1, width),
        qk_weight.reshape(NZ, NX * width, heads),
    )
    return stream.T, queries_keys


def solution(mesh):
    placed = (P(None, "row"), P("row", "col"), P("row", "col"), P("col"), P(None, "col"))
    return jax.shard_map(
        per_device,
        mesh=mesh,
        in_specs=placed,
        out_specs=(P("row", "col"), P("row", "col")),
        check_vma=False,
    )
```

```python
import functools

import jax
import jax.numpy as jnp
from jax import lax
from jax.experimental import pallas as pl
from jax.experimental.pallas import tpu as pltpu
from jax.sharding import PartitionSpec as P

MESH = pl.DeviceIdType.MESH
F32, BF16 = jnp.float32, jnp.bfloat16
NX, NZ, NY = 4, 8, 4
ROWS, COLS = 2 * NY, NZ * NX
TOK = 128
X_FIRST = 48
STEPS_Z = (1, -1, 2, -2, 3, -3, 4)
STEPS_X = (1, -1, 2)


def merge(stats, count):
    means, squares = stats[:, 0], stats[:, 1]
    mean = jnp.mean(means, axis=0, keepdims=True)
    off = means - mean
    square = jnp.sum(squares, axis=0, keepdims=True) + count * jnp.sum(off * off, axis=0, keepdims=True)
    return jnp.concatenate([mean, square], axis=0)


def kernel(
    hidden, down, residual, gain, weight, stream_out, qk_out,
    hid_v, down_v, res_v, gain_in, gains, gain_rows, w_v, qk_v,
    rs_send, rs_recv, g, stats_z, stats_x,
    load_sem, rs_ssem, rs_rsem, gx_ssem, gx_rsem, gz_ssem, gz_rsem,
    sx_ssem, sx_rsem, sz_ssem, sz_rsem,
    a_rsem, bx_rsem, bz_rsem, ag_ssem,
):
    row, col = lax.axis_index("row"), lax.axis_index("col")
    y, core = row // 2, row % 2
    z, x = col // NX, col % NX
    wide = down.shape[0]

    def at(zz, xx):
        return (row, zz * NX + xx)

    def zs(d):
        return lax.rem(z + d + NZ, NZ)

    def xs(d):
        return lax.rem(x + d + NX, NX)

    def load(src, dst, sem):
        copy = pltpu.make_async_copy(src, dst, load_sem.at[sem])
        copy.start()
        return copy

    c_gain = load(gain, gain_in, 6)
    c_down = load(down, down_v, 0)
    c_hid = []
    order = (2, 1, 3, 0)
    for i, d in enumerate(order):
        rows = pl.ds(pl.multiple_of(lax.rem(y + d, NY) * 2 * TOK, 2 * TOK), 2 * TOK)
        c_hid.append(load(hidden.at[rows], hid_v.at[i], 2 + i))
    c_res = load(residual, res_v, 7)

    barrier = pltpu.get_barrier_semaphore()
    peers = [(lax.rem(row + d, ROWS), col) for d in range(1, ROWS)]
    peers += [at(z, xs(d)) for d in STEPS_X]
    peers += [at(zs(d), x) for d in STEPS_Z]
    for peer in peers:
        pl.semaphore_signal(barrier, inc=1, device_id=peer, device_id_type=MESH)

    sends = []

    def send(src, dst, ssem, rsem, peer):
        copy = pltpu.make_async_remote_copy(
            src_ref=src, dst_ref=dst, send_sem=ssem, recv_sem=rsem,
            device_id=peer, device_id_type=MESH,
        )
        copy.start()
        return copy

    def arrived(ref, rsem):
        pltpu.make_async_copy(ref, ref, rsem).wait()

    def over_x(ref, ssem, rsem):
        for i, d in enumerate(STEPS_X):
            sends.append(send(ref, ref, ssem.at[i], rsem.at[x], at(z, xs(d))))

    def over_z(ref, ssem, rsem):
        for i, d in enumerate(STEPS_Z):
            sends.append(send(ref, ref, ssem.at[i], rsem.at[z], at(zs(d), x)))

    def project(i):
        c_hid[i].wait()
        part = lax.dot_general(
            down_v[...], hid_v[i], (((1,), (1,)), ((), ())), preferred_element_type=F32
        ).astype(BF16)
        for k in range(2):
            rs_send[2 * i + k] = part[:, k * TOK:(k + 1) * TOK]

    def leave(i):
        yy = lax.rem(y + order[i], NY)
        for k in range(2):
            piece = rs_send.at[2 * i + k]
            peer = (yy * 2 + k, col)
            if order[i]:
                sends.append(send(piece, rs_recv.at[row], rs_ssem.at[2 * i + k], rs_rsem.at[row], peer))
            else:
                @pl.when(core != k)
                def _():
                    send(piece, rs_recv.at[row], rs_ssem.at[2 * i + k], rs_rsem.at[row], peer)

                @pl.when(core == k)
                def _():
                    rs_recv[row] = piece[...]

    c_down.wait()
    project(0)
    c_gain.wait()
    gains[col] = gain_in[...].astype(F32).reshape(1, wide)
    pl.semaphore_wait(barrier, len(peers))
    leave(0)
    over_x(gains.at[col], gx_ssem, gx_rsem)
    for i in range(1, NY):
        project(i)
        leave(i)

    c_w = load(weight, w_v, 8)

    for d in STEPS_X:
        arrived(gains.at[z * NX + xs(d)], gx_rsem.at[xs(d)])
    over_z(gains.at[pl.ds(z * NX, NX)], gz_ssem, gz_rsem)
    for d in STEPS_Z:
        arrived(gains.at[pl.ds(zs(d) * NX, NX)], gz_rsem.at[zs(d)])
    for c in range(NZ):
        gain_rows[c] = jnp.concatenate([gains[c * NX + k] for k in range(NX)], axis=1)

    for d in range(1, ROWS):
        r = lax.rem(row + d, ROWS)
        arrived(rs_recv.at[r], rs_rsem.at[r])
    c_res.wait()
    total = rs_recv[0].astype(F32)
    for r in range(1, ROWS):
        total = total + rs_recv[r].astype(F32)
    stream = (res_v[...].astype(F32) + total).astype(BF16)
    g[col] = stream

    last = pl.ds(X_FIRST, wide - X_FIRST)
    first = pl.ds(0, X_FIRST)
    count = [0]

    def push(ref, rsem, peer):
        sends.append(send(ref, ref, ag_ssem.at[count[0]], rsem, peer))
        count[0] += 1

    def push_x(dz):
        slot = zs(dz) * NX + x
        for e in STEPS_X:
            push(g.at[slot, last], a_rsem.at[slot], at(z, xs(e)))

    def group(dz):
        return g.at[pl.ds(zs(dz) * NX, NX), first]

    for e in STEPS_X:
        push(g.at[col, first], bx_rsem.at[x], at(z, xs(e)))
    for d in STEPS_Z:
        push(g.at[col, last], a_rsem.at[col], at(zs(d), x))

    push_x(0)

    values = stream.astype(F32)
    mean = jnp.mean(values, axis=0, keepdims=True)
    off = values - mean
    stats_z[z] = jnp.concatenate([mean, jnp.sum(off * off, axis=0, keepdims=True)], axis=0)
    over_z(stats_z.at[z], sz_ssem, sz_rsem)
    stream_out[...] = stream

    for e in STEPS_X:
        arrived(g.at[z * NX + xs(e), first], bx_rsem.at[xs(e)])
    for d in (4, 3, -3, 2, -2, 1, -1):
        push(group(0), bz_rsem.at[z], at(zs(d), x))

    def from_z(d):
        slot = zs(d) * NX + x
        arrived(g.at[slot, last], a_rsem.at[slot])
        push_x(d)

    for d in STEPS_Z[:4]:
        from_z(d)
    for d in STEPS_Z:
        arrived(stats_z.at[zs(d)], sz_rsem.at[zs(d)])
    stats_x[x] = merge(stats_z[...], wide)
    over_x(stats_x.at[x], sx_ssem, sx_rsem)
    for d in STEPS_Z[4:]:
        from_z(d)

    for e in STEPS_X:
        arrived(stats_x.at[xs(e)], sx_rsem.at[xs(e)])
    both = merge(stats_x[...], NZ * wide)
    scale = 1.0 / jnp.sqrt(both[1:] * (1.0 / (COLS * wide)) + 1e-6)
    mean_t = jnp.transpose(jnp.broadcast_to(both[:1], (TOK, TOK)))
    scale_t = jnp.transpose(jnp.broadcast_to(scale, (TOK, TOK)))
    c_w.wait()

    for i, d in enumerate((0,) + STEPS_Z):
        for e in STEPS_X:
            slot = zs(d) * NX + xs(e)
            arrived(g.at[slot, last], a_rsem.at[slot])
        if d:
            arrived(group(d), bz_rsem.at[zs(d)])
        zz = zs(d)
        block = g[pl.ds(zz * NX, NX)].reshape(NX * wide, TOK)
        tokens = jnp.transpose(block)
        row_gain = gain_rows[zz]
        pieces = []
        for k in range(NX * wide // TOK):
            lanes = slice(k * TOK, (k + 1) * TOK)
            piece = (tokens[:, lanes].astype(F32) - mean_t) * scale_t * row_gain[:, lanes]
            pieces.append(piece.astype(BF16))
        out = jnp.dot(jnp.concatenate(pieces, axis=1), w_v[zz], preferred_element_type=F32)
        if i == 0:
            qk_v[...] = out
        elif i < NZ - 1:
            qk_v[...] += out
        else:
            qk_out[...] = (qk_v[...] + out).astype(BF16)

    for copy in sends:
        copy.wait_send()
    for k in range(2):
        @pl.when(core != k)
        def _():
            pltpu.make_async_copy(rs_send.at[6 + k], rs_send.at[6 + k], rs_ssem.at[6 + k]).wait()


def deliver(stream, queries_keys, stream_out, qk_out, sem):
    copies = [
        pltpu.make_async_copy(stream, stream_out, sem.at[0]),
        pltpu.make_async_copy(queries_keys, qk_out, sem.at[1]),
    ]
    for copy in copies:
        copy.start()
    for copy in copies:
        copy.wait()


def per_device(hidden, down_weight, residual, gain, qk_weight):
    depth, width = down_weight.shape
    full, heads = qk_weight.shape
    vmem_spec = pl.BlockSpec(memory_space=pltpu.VMEM)
    any_spec = pl.BlockSpec(memory_space=pl.ANY)
    dma = pltpu.SemaphoreType.DMA
    stream, queries_keys = pl.pallas_call(
        kernel,
        out_shape=(pltpu.VMEM((width, TOK), BF16), pltpu.VMEM((TOK, heads), BF16)),
        in_specs=[any_spec] * 5,
        out_specs=(vmem_spec, vmem_spec),
        scratch_shapes=[
            pltpu.VMEM((NY, 2 * TOK, depth), BF16),
            pltpu.VMEM((width, depth), BF16),
            pltpu.VMEM((width, TOK), BF16),
            pltpu.VMEM((width,), BF16),
            pltpu.VMEM((COLS, 1, width), F32),
            pltpu.VMEM((NZ, 1, NX * width), F32),
            pltpu.VMEM((NZ, NX * width, heads), BF16),
            pltpu.VMEM((TOK, heads), F32),
            pltpu.VMEM((ROWS, width, TOK), BF16),
            pltpu.VMEM((ROWS, width, TOK), BF16),
            pltpu.VMEM((COLS, width, TOK), BF16),
            pltpu.VMEM((NZ, 2, TOK), F32),
            pltpu.VMEM((NX, 2, TOK), F32),
            dma((9,)),
            dma((ROWS,)), dma((ROWS,)),
            dma((NX - 1,)), dma((NX,)), dma((NZ - 1,)), dma((NZ,)),
            dma((NX - 1,)), dma((NX,)), dma((NZ - 1,)), dma((NZ,)),
            dma((COLS,)), dma((NX,)), dma((NZ,)),
            dma((48,)),
        ],
        compiler_params=pltpu.CompilerParams(
            collective_id=0, has_side_effects=True, vmem_limit_bytes=56 * 1024 * 1024
        ),
    )(
        hidden, down_weight.T, residual.T, gain,
        qk_weight.reshape(NZ, NX * width, heads),
    )
    stream, queries_keys = pl.pallas_call(
        deliver,
        out_shape=(
            jax.ShapeDtypeStruct((width, TOK), BF16),
            jax.ShapeDtypeStruct((TOK, heads), BF16),
        ),
        in_specs=[vmem_spec] * 2,
        out_specs=(any_spec, any_spec),
        scratch_shapes=[dma((2,))],
    )(
        pltpu.with_memory_space_constraint(stream, pltpu.VMEM),
        pltpu.with_memory_space_constraint(queries_keys, pltpu.VMEM),
    )
    return stream.T, queries_keys


def solution(mesh):
    placed = (P(None, "row"), P("row", "col"), P("row", "col"), P("col"), P(None, "col"))
    return jax.shard_map(
        per_device,
        mesh=mesh,
        in_specs=placed,
        out_specs=(P("row", "col"), P("row", "col")),
        check_vma=False,
    )
```

```python
import functools

import jax
import jax.numpy as jnp
from jax import lax
from jax.experimental import pallas as pl
from jax.experimental.pallas import tpu as pltpu
from jax.sharding import PartitionSpec as P

MESH = pl.DeviceIdType.MESH
F32, BF16 = jnp.float32, jnp.bfloat16
NX, NZ, NY = 4, 8, 4
ROWS, COLS = 2 * NY, NZ * NX
TOK = 128
X_FIRST = 48
STEPS_Z = (1, -1, 2, -2, 3, -3, 4)
STEPS_X = (1, -1, 2)


def merge(stats, count):
    means, squares = stats[:, 0], stats[:, 1]
    mean = jnp.mean(means, axis=0, keepdims=True)
    off = means - mean
    square = jnp.sum(squares, axis=0, keepdims=True) + count * jnp.sum(off * off, axis=0, keepdims=True)
    return jnp.concatenate([mean, square], axis=0)


def kernel(
    hidden, down, residual, gain, weight, stream_out, qk_out,
    hid_v, down_v, res_v, gain_in, gains, gain_rows, w_v, qk_v,
    pair_send, pair_recv, rs_send, rs_recv, g, stats_z, stats_x,
    load_sem, pair_ssem, pair_rsem, rs_ssem, rs_rsem, gx_ssem, gx_rsem, gz_ssem, gz_rsem,
    sx_ssem, sx_rsem, sz_ssem, sz_rsem,
    a_rsem, bx_rsem, bz_rsem, ag_ssem,
):
    row, col = lax.axis_index("row"), lax.axis_index("col")
    y, core = row // 2, row % 2
    z, x = col // NX, col % NX
    wide = down.shape[0]

    def at(zz, xx):
        return (row, zz * NX + xx)

    def zs(d):
        return lax.rem(z + d + NZ, NZ)

    def xs(d):
        return lax.rem(x + d + NX, NX)

    def load(src, dst, sem):
        copy = pltpu.make_async_copy(src, dst, load_sem.at[sem])
        copy.start()
        return copy

    order = (2, 1), (3, 0)
    parts = [(1 - core, order[0]), (1 - core, order[1]), (core, order[0]), (core, order[1])]

    def load_hidden(i):
        owner, places = parts[i]
        copies = []
        for k, d in enumerate(places):
            first_row = (lax.rem(y + d, NY) * 2 + owner) * TOK
            rows = pl.ds(pl.multiple_of(first_row, TOK), TOK)
            copies.append(load(hidden.at[rows], hid_v.at[i, pl.ds(k * TOK, TOK)], 8 + 2 * i + k))
        return copies

    c_gain = load(gain, gain_in, 1)
    c_down = load(down, down_v, 0)
    c_hid = [load_hidden(0)]

    barrier = pltpu.get_barrier_semaphore()
    sibling = (y * 2 + 1 - core, col)
    peers = [sibling] + [(lax.rem(y + d, NY) * 2 + core, col) for d in range(1, NY)]
    peers += [at(z, xs(d)) for d in STEPS_X]
    peers += [at(zs(d), x) for d in STEPS_Z]
    for peer in peers:
        pl.semaphore_signal(barrier, inc=1, device_id=peer, device_id_type=MESH)

    sends = []

    def send(src, dst, ssem, rsem, peer):
        copy = pltpu.make_async_remote_copy(
            src_ref=src, dst_ref=dst, send_sem=ssem, recv_sem=rsem,
            device_id=peer, device_id_type=MESH,
        )
        copy.start()
        return copy

    def arrived(ref, rsem):
        pltpu.make_async_copy(ref, ref, rsem).wait()

    def over_x(ref, ssem, rsem):
        for i, d in enumerate(STEPS_X):
            sends.append(send(ref, ref, ssem.at[i], rsem.at[x], at(z, xs(d))))

    def over_z(ref, ssem, rsem):
        for i, d in enumerate(STEPS_Z):
            sends.append(send(ref, ref, ssem.at[i], rsem.at[z], at(zs(d), x)))

    def project(i):
        for copy in c_hid[i]:
            copy.wait()
        if i + 2 < NY:
            c_hid.append(load_hidden(i + 2))
        return lax.dot_general(
            down_v[...], hid_v[i], (((1,), (1,)), ((), ())), preferred_element_type=F32
        )

    def to_sibling(i):
        for k in range(2):
            j = 2 * i + k
            sends.append(send(pair_send.at[j], pair_recv.at[j], pair_ssem.at[j], pair_rsem.at[j], sibling))

    def hand(i):
        part = project(i).astype(BF16)
        for k in range(2):
            pair_send[2 * i + k] = part[:, k * TOK:(k + 1) * TOK]

    c_down.wait()
    c_hid.append(load_hidden(1))
    hand(0)
    c_gain.wait()
    gains[col] = gain_in[...].astype(F32).reshape(1, wide)
    pl.semaphore_wait(barrier, len(peers))
    to_sibling(0)
    over_x(gains.at[col], gx_ssem, gx_rsem)
    hand(1)
    to_sibling(1)
    c_res = load(residual, res_v, 2)
    own = None
    for i in range(2):
        part = project(2 + i)
        for k in range(2):
            j, d = 2 * i + k, order[i][k]
            arrived(pair_recv.at[j], pair_rsem.at[j])
            both = part[:, k * TOK:(k + 1) * TOK] + pair_recv[j].astype(F32)
            if d:
                rs_send[d - 1] = both.astype(BF16)
                peer = (lax.rem(y + d, NY) * 2 + core, col)
                sends.append(send(rs_send.at[d - 1], rs_recv.at[NY - 1 - d], rs_ssem.at[d - 1], rs_rsem.at[NY - 1 - d], peer))
            else:
                own = both

    c_w = load(weight, w_v, 3)

    for d in STEPS_X:
        arrived(gains.at[z * NX + xs(d)], gx_rsem.at[xs(d)])
    over_z(gains.at[pl.ds(z * NX, NX)], gz_ssem, gz_rsem)
    c_res.wait()
    total = res_v[...].astype(F32) + own
    for d in range(NY - 1):
        arrived(rs_recv.at[d], rs_rsem.at[d])
        total = total + rs_recv[d].astype(F32)
    stream = total.astype(BF16)
    g[col] = stream

    last = pl.ds(X_FIRST, wide - X_FIRST)
    first = pl.ds(0, X_FIRST)
    count = [0]

    def push(ref, rsem, peer):
        sends.append(send(ref, ref, ag_ssem.at[count[0]], rsem, peer))
        count[0] += 1

    def push_x(dz):
        slot = zs(dz) * NX + x
        for e in STEPS_X:
            push(g.at[slot, last], a_rsem.at[slot], at(z, xs(e)))

    def group(dz):
        return g.at[pl.ds(zs(dz) * NX, NX), first]

    for e in STEPS_X:
        push(g.at[col, first], bx_rsem.at[x], at(z, xs(e)))
    for d in STEPS_Z:
        push(g.at[col, last], a_rsem.at[col], at(zs(d), x))

    push_x(0)

    values = stream.astype(F32)
    mean = jnp.mean(values, axis=0, keepdims=True)
    off = values - mean
    stats_z[z] = jnp.concatenate([mean, jnp.sum(off * off, axis=0, keepdims=True)], axis=0)
    over_z(stats_z.at[z], sz_ssem, sz_rsem)
    stream_out[...] = stream

    for e in STEPS_X:
        arrived(g.at[z * NX + xs(e), first], bx_rsem.at[xs(e)])
    for d in (4, 3, -3, 2, -2, 1, -1):
        push(group(0), bz_rsem.at[z], at(zs(d), x))

    def from_z(d):
        slot = zs(d) * NX + x
        arrived(g.at[slot, last], a_rsem.at[slot])
        push_x(d)

    for d in STEPS_Z[:4]:
        from_z(d)
    for d in STEPS_Z:
        arrived(stats_z.at[zs(d)], sz_rsem.at[zs(d)])
    stats_x[x] = merge(stats_z[...], wide)
    over_x(stats_x.at[x], sx_ssem, sx_rsem)
    for d in STEPS_Z[4:]:
        from_z(d)

    for d in STEPS_Z:
        arrived(gains.at[pl.ds(zs(d) * NX, NX)], gz_rsem.at[zs(d)])
    for c in range(NZ):
        gain_rows[c] = jnp.concatenate([gains[c * NX + k] for k in range(NX)], axis=1)

    for e in STEPS_X:
        arrived(stats_x.at[xs(e)], sx_rsem.at[xs(e)])
    both = merge(stats_x[...], NZ * wide)
    scale = 1.0 / jnp.sqrt(both[1:] * (1.0 / (COLS * wide)) + 1e-6)
    mean_t = jnp.transpose(jnp.broadcast_to(both[:1], (TOK, TOK)))
    scale_t = jnp.transpose(jnp.broadcast_to(scale, (TOK, TOK)))
    c_w.wait()

    for i, d in enumerate((0,) + STEPS_Z):
        for e in STEPS_X:
            slot = zs(d) * NX + xs(e)
            arrived(g.at[slot, last], a_rsem.at[slot])
        if d:
            arrived(group(d), bz_rsem.at[zs(d)])
        zz = zs(d)
        block = g[pl.ds(zz * NX, NX)].reshape(NX * wide, TOK)
        tokens = jnp.transpose(block)
        row_gain = gain_rows[zz]
        pieces = []
        for k in range(NX * wide // TOK):
            lanes = slice(k * TOK, (k + 1) * TOK)
            piece = (tokens[:, lanes].astype(F32) - mean_t) * scale_t * row_gain[:, lanes]
            pieces.append(piece.astype(BF16))
        out = jnp.dot(jnp.concatenate(pieces, axis=1), w_v[zz], preferred_element_type=F32)
        if i == 0:
            qk_v[...] = out
        elif i < NZ - 1:
            qk_v[...] += out
        else:
            qk_out[...] = (qk_v[...] + out).astype(BF16)

    for copy in sends:
        copy.wait_send()


def deliver(stream, queries_keys, stream_out, qk_out, sem):
    copies = [
        pltpu.make_async_copy(stream, stream_out, sem.at[0]),
        pltpu.make_async_copy(queries_keys, qk_out, sem.at[1]),
    ]
    for copy in copies:
        copy.start()
    for copy in copies:
        copy.wait()


def per_device(hidden, down_weight, residual, gain, qk_weight):
    depth, width = down_weight.shape
    full, heads = qk_weight.shape
    vmem_spec = pl.BlockSpec(memory_space=pltpu.VMEM)
    any_spec = pl.BlockSpec(memory_space=pl.ANY)
    dma = pltpu.SemaphoreType.DMA
    stream, queries_keys = pl.pallas_call(
        kernel,
        out_shape=(pltpu.VMEM((width, TOK), BF16), pltpu.VMEM((TOK, heads), BF16)),
        in_specs=[any_spec] * 5,
        out_specs=(vmem_spec, vmem_spec),
        scratch_shapes=[
            pltpu.VMEM((NY, 2 * TOK, depth), BF16),
            pltpu.VMEM((width, depth), BF16),
            pltpu.VMEM((width, TOK), BF16),
            pltpu.VMEM((width,), BF16),
            pltpu.VMEM((COLS, 1, width), F32),
            pltpu.VMEM((NZ, 1, NX * width), F32),
            pltpu.VMEM((NZ, NX * width, heads), BF16),
            pltpu.VMEM((TOK, heads), F32),
            pltpu.VMEM((NY, width, TOK), BF16),
            pltpu.VMEM((NY, width, TOK), BF16),
            pltpu.VMEM((NY - 1, width, TOK), BF16),
            pltpu.VMEM((NY - 1, width, TOK), BF16),
            pltpu.VMEM((COLS, width, TOK), BF16),
            pltpu.VMEM((NZ, 2, TOK), F32),
            pltpu.VMEM((NX, 2, TOK), F32),
            dma((16,)),
            dma((NY,)), dma((NY,)), dma((NY - 1,)), dma((NY - 1,)),
            dma((NX - 1,)), dma((NX,)), dma((NZ - 1,)), dma((NZ,)),
            dma((NX - 1,)), dma((NX,)), dma((NZ - 1,)), dma((NZ,)),
            dma((COLS,)), dma((NX,)), dma((NZ,)),
            dma((48,)),
        ],
        compiler_params=pltpu.CompilerParams(
            collective_id=0, has_side_effects=True, vmem_limit_bytes=56 * 1024 * 1024
        ),
    )(
        hidden, down_weight.T, residual.T, gain,
        qk_weight.reshape(NZ, NX * width, heads),
    )
    stream, queries_keys = pl.pallas_call(
        deliver,
        out_shape=(
            jax.ShapeDtypeStruct((width, TOK), BF16),
            jax.ShapeDtypeStruct((TOK, heads), BF16),
        ),
        in_specs=[vmem_spec] * 2,
        out_specs=(any_spec, any_spec),
        scratch_shapes=[dma((2,))],
    )(
        pltpu.with_memory_space_constraint(stream, pltpu.VMEM),
        pltpu.with_memory_space_constraint(queries_keys, pltpu.VMEM),
    )
    return stream.T, queries_keys


def solution(mesh):
    placed = (P(None, "row"), P("row", "col"), P("row", "col"), P("col"), P(None, "col"))
    return jax.shard_map(
        per_device,
        mesh=mesh,
        in_specs=placed,
        out_specs=(P("row", "col"), P("row", "col")),
        check_vma=False,
    )
```

```python
import functools

import jax
import jax.numpy as jnp
from jax import lax
from jax.experimental import pallas as pl
from jax.experimental.pallas import tpu as pltpu
from jax.sharding import PartitionSpec as P

MESH = pl.DeviceIdType.MESH
F32, BF16 = jnp.float32, jnp.bfloat16
NX, NZ, NY = 4, 8, 4
ROWS, COLS = 2 * NY, NZ * NX
TOK = 128
X_FIRST = 48
STEPS_Z = (1, -1, 2, -2, 3, -3, 4)
STEPS_X = (1, -1, 2)

SHARE_AT = 12
MERGE_AT = ("z", -3)
ORDER = (
    ("s", "z", 1), ("s", "z", -1), ("s", "bx", 2), ("s", "x", 0, -1), ("s", "bx", -1), ("s", "z", 2), ("s", "z", 3),
    ("s", "bx", 1), ("s", "z", -3), ("s", "z", -2), ("s", "x", 0, 2), ("s", "x", 0, 1), ("w", "z", 1),
    ("s", "x", 1, 2), ("w", "z", -1), ("w", "bx", 1), ("s", "x", 1, -1), ("s", "x", 1, 1), ("s", "x", -1, 2),
    ("s", "x", -1, -1), ("w", "bx", 2), ("w", "bx", -1), ("s", "bz", -3), ("s", "bz", 3), ("s", "bz", -1),
    ("s", "x", -1, 1), ("s", "bz", 1), ("w", "z", 2), ("s", "x", 2, 2), ("s", "x", 2, 1), ("s", "x", 2, -1),
    ("w", "z", 3), ("s", "x", 3, 1), ("w", "z", -3), ("s", "z4", 3), ("s", "x", -3, -1), ("w", "z", -2),
    ("s", "z4", -3), ("s", "bz", 2), ("s", "bz", -2), ("s", "x", 3, 2), ("s", "x", -2, 1), ("s", "x", -2, -1),
    ("s", "bz", 4), ("w", "x", -1, 2), ("s", "x", -3, 2), ("w", "x", 1, -1), ("w", "bz", -1), ("s", "x", -3, 1),
    ("s", "x", 3, -1), ("w", "bz", 1), ("s", "x", -2, 2), ("w", "x", 0, 1), ("w", "x", -1, -1), ("w", "bz", -3),
    ("w", "x", 2, 1), ("w", "x", 0, -1), ("w", "x", 1, 1), ("w", "z4", 3), ("w", "x", -3, -1), ("w", "x", 3, 1),
    ("w", "x", 2, 2), ("w", "z4", -3), ("w", "bz", 3), ("s", "x", 4, 2), ("w", "x", 0, 2), ("c", 0),
    ("s", "x", 4, 1), ("s", "x", 4, -1), ("w", "x", 1, 2), ("w", "x", -2, 1), ("c", 1), ("w", "x", -1, 1),
    ("w", "x", -2, -1), ("c", -1), ("w", "x", 3, 2), ("w", "x", 2, -1), ("w", "x", 3, -1), ("c", 3),
    ("w", "x", -3, 1), ("w", "x", -3, 2), ("c", -3), ("w", "bz", -2), ("w", "bz", 2), ("c", 2), ("w", "x", -2, 2),
    ("c", -2), ("w", "x", 4, 1), ("w", "bz", 4), ("w", "x", 4, -1), ("w", "x", 4, 2), ("c", 4),
)


def merge(stats, count):
    means, squares = stats[:, 0], stats[:, 1]
    mean = jnp.mean(means, axis=0, keepdims=True)
    off = means - mean
    square = jnp.sum(squares, axis=0, keepdims=True) + count * jnp.sum(off * off, axis=0, keepdims=True)
    return jnp.concatenate([mean, square], axis=0)


def kernel(
    hidden, down, residual, gain, weight, stream_out, qk_out,
    hid_v, down_v, res_v, gain_in, gains, gain_rows, w_v, qk_v,
    pair_send, pair_recv, rs_send, rs_recv, g, stats_z, stats_x,
    load_sem, pair_ssem, pair_rsem, rs_ssem, rs_rsem, gx_ssem, gx_rsem, gz_ssem, gz_rsem,
    sx_ssem, sx_rsem, sz_ssem, sz_rsem,
    ag_ssem, ag_rsem,
):
    row, col = lax.axis_index("row"), lax.axis_index("col")
    y, core = row // 2, row % 2
    z, x = col // NX, col % NX
    wide = down.shape[0]

    def at(zz, xx):
        return (row, zz * NX + xx)

    def zs(d):
        return lax.rem(z + d + NZ, NZ)

    def xs(d):
        return lax.rem(x + d + NX, NX)

    def load(src, dst, sem):
        copy = pltpu.make_async_copy(src, dst, load_sem.at[sem])
        copy.start()
        return copy

    order = (2, 1), (3, 0)
    parts = [(1 - core, order[0]), (1 - core, order[1]), (core, order[0]), (core, order[1])]

    def load_hidden(i):
        owner, places = parts[i]
        copies = []
        for k, d in enumerate(places):
            first_row = (lax.rem(y + d, NY) * 2 + owner) * TOK
            rows = pl.ds(pl.multiple_of(first_row, TOK), TOK)
            copies.append(load(hidden.at[rows], hid_v.at[i, pl.ds(k * TOK, TOK)], 8 + 2 * i + k))
        return copies

    c_gain = load(gain, gain_in, 1)
    c_down = load(down, down_v, 0)
    c_hid = [load_hidden(0)]

    barrier = pltpu.get_barrier_semaphore()
    sibling = (y * 2 + 1 - core, col)
    peers = [sibling] + [(lax.rem(y + d, NY) * 2 + core, col) for d in range(1, NY)]
    peers += [at(z, xs(d)) for d in STEPS_X]
    peers += [at(zs(d), x) for d in STEPS_Z]
    for peer in peers:
        pl.semaphore_signal(barrier, inc=1, device_id=peer, device_id_type=MESH)

    sends = []

    def send(src, dst, ssem, rsem, peer):
        copy = pltpu.make_async_remote_copy(
            src_ref=src, dst_ref=dst, send_sem=ssem, recv_sem=rsem,
            device_id=peer, device_id_type=MESH,
        )
        copy.start()
        return copy

    def arrived(ref, rsem):
        pltpu.make_async_copy(ref, ref, rsem).wait()

    def over_x(ref, ssem, rsem):
        for i, d in enumerate(STEPS_X):
            sends.append(send(ref, ref, ssem.at[i], rsem.at[x], at(z, xs(d))))

    def over_z(ref, ssem, rsem):
        for i, d in enumerate(STEPS_Z):
            sends.append(send(ref, ref, ssem.at[i], rsem.at[z], at(zs(d), x)))

    def project(i):
        for copy in c_hid[i]:
            copy.wait()
        if i + 2 < NY:
            c_hid.append(load_hidden(i + 2))
        return lax.dot_general(
            down_v[...], hid_v[i], (((1,), (1,)), ((), ())), preferred_element_type=F32
        )

    def to_sibling(i):
        for k in range(2):
            j = 2 * i + k
            sends.append(send(pair_send.at[j], pair_recv.at[j], pair_ssem.at[j], pair_rsem.at[j], sibling))

    def hand(i):
        part = project(i).astype(BF16)
        for k in range(2):
            pair_send[2 * i + k] = part[:, k * TOK:(k + 1) * TOK]

    c_down.wait()
    c_hid.append(load_hidden(1))
    hand(0)
    c_gain.wait()
    gains[col] = gain_in[...].astype(F32).reshape(1, wide)
    pl.semaphore_wait(barrier, len(peers))
    to_sibling(0)
    over_x(gains.at[col], gx_ssem, gx_rsem)
    hand(1)
    to_sibling(1)
    c_res = load(residual, res_v, 2)
    own = None
    for i in range(2):
        part = project(2 + i)
        for k in range(2):
            j, d = 2 * i + k, order[i][k]
            arrived(pair_recv.at[j], pair_rsem.at[j])
            both = part[:, k * TOK:(k + 1) * TOK] + pair_recv[j].astype(F32)
            if d:
                rs_send[d - 1] = both.astype(BF16)
                peer = (lax.rem(y + d, NY) * 2 + core, col)
                sends.append(send(rs_send.at[d - 1], rs_recv.at[NY - 1 - d], rs_ssem.at[d - 1], rs_rsem.at[NY - 1 - d], peer))
            else:
                own = both

    c_w = load(weight, w_v, 3)

    for d in STEPS_X:
        arrived(gains.at[z * NX + xs(d)], gx_rsem.at[xs(d)])
    over_z(gains.at[pl.ds(z * NX, NX)], gz_ssem, gz_rsem)
    c_res.wait()
    total = res_v[...].astype(F32) + own
    for d in range(NY - 1):
        arrived(rs_recv.at[d], rs_rsem.at[d])
        total = total + rs_recv[d].astype(F32)
    stream = total.astype(BF16)
    g[col] = stream

    last = pl.ds(X_FIRST, wide - X_FIRST)
    first = pl.ds(0, X_FIRST)
    middle = X_FIRST + 64
    halves = {3: pl.ds(X_FIRST, 64), -3: pl.ds(middle, wide - middle)}

    def place(dz, dx):
        return zs(dz) * NX + xs(dx)

    def group(dz):
        return g.at[pl.ds(zs(dz) * NX, NX), first]

    def sent(kind, step):
        if kind == "z":
            return g.at[col, last], at(zs(step[0]), x)
        if kind == "z4":
            return g.at[place(-step[0], 0), halves[step[0]]], at(zs(step[0] // 3), x)
        if kind == "bx":
            return g.at[col, first], at(z, xs(step[0]))
        if kind == "bz":
            return group(0), at(zs(step[0]), x)
        return g.at[place(-step[0], 0), last], at(z, xs(step[1]))

    def received(kind, step):
        if kind == "z":
            return g.at[place(-step[0], 0), last]
        if kind == "z4":
            return g.at[place(4, 0), halves[step[0]]]
        if kind == "bx":
            return g.at[place(0, -step[0]), first]
        if kind == "bz":
            return group(-step[0])
        return g.at[place(-step[0], -step[1]), last]

    copies = [op[1:] for op in ORDER if op[0] == "s"]
    computes = [op[1] for op in ORDER if op[0] == "c"]

    def share_statistics():
        values = stream.astype(F32)
        mean = jnp.mean(values, axis=0, keepdims=True)
        off = values - mean
        stats_z[z] = jnp.concatenate([mean, jnp.sum(off * off, axis=0, keepdims=True)], axis=0)
        over_z(stats_z.at[z], sz_ssem, sz_rsem)
        stream_out[...] = stream

    def merge_statistics():
        for d in STEPS_Z:
            arrived(stats_z.at[zs(d)], sz_rsem.at[zs(d)])
        stats_x[x] = merge(stats_z[...], wide)
        over_x(stats_x.at[x], sx_ssem, sx_rsem)

    def before_compute():
        for d in STEPS_Z:
            arrived(gains.at[pl.ds(zs(d) * NX, NX)], gz_rsem.at[zs(d)])
        for c in range(NZ):
            gain_rows[c] = jnp.concatenate([gains[c * NX + k] for k in range(NX)], axis=1)
        for e in STEPS_X:
            arrived(stats_x.at[xs(e)], sx_rsem.at[xs(e)])
        both = merge(stats_x[...], NZ * wide)
        scale = 1.0 / jnp.sqrt(both[1:] * (1.0 / (COLS * wide)) + 1e-6)
        mean_t = jnp.transpose(jnp.broadcast_to(both[:1], (TOK, TOK)))
        scale_t = jnp.transpose(jnp.broadcast_to(scale, (TOK, TOK)))
        c_w.wait()
        return mean_t, scale_t

    def project_group(d, mean_t, scale_t):
        zz = zs(-d)
        block = g[pl.ds(zz * NX, NX)].reshape(NX * wide, TOK)
        tokens = jnp.transpose(block)
        row_gain = gain_rows[zz]
        pieces = []
        for k in range(NX * wide // TOK):
            lanes = slice(k * TOK, (k + 1) * TOK)
            piece = (tokens[:, lanes].astype(F32) - mean_t) * scale_t * row_gain[:, lanes]
            pieces.append(piece.astype(BF16))
        out = jnp.dot(jnp.concatenate(pieces, axis=1), w_v[zz], preferred_element_type=F32)
        if d == computes[0]:
            qk_v[...] = out
        elif d != computes[-1]:
            qk_v[...] += out
        else:
            qk_out[...] = (qk_v[...] + out).astype(BF16)

    moments = None
    started = 0
    for op, kind, *step in ORDER:
        if op == "c":
            if moments is None:
                moments = before_compute()
            project_group(kind, *moments)
            continue
        number = copies.index((kind, *step))
        if op == "s":
            ref, peer = sent(kind, step)
            sends.append(send(ref, ref, ag_ssem.at[number], ag_rsem.at[number], peer))
            started += 1
            if started == SHARE_AT:
                share_statistics()
        else:
            arrived(received(kind, step), ag_rsem.at[number])
            if (kind, *step) == MERGE_AT:
                merge_statistics()

    for copy in sends:
        copy.wait_send()


def deliver(stream, queries_keys, stream_out, qk_out, sem):
    copies = [
        pltpu.make_async_copy(stream, stream_out, sem.at[0]),
        pltpu.make_async_copy(queries_keys, qk_out, sem.at[1]),
    ]
    for copy in copies:
        copy.start()
    for copy in copies:
        copy.wait()


def per_device(hidden, down_weight, residual, gain, qk_weight):
    depth, width = down_weight.shape
    full, heads = qk_weight.shape
    vmem_spec = pl.BlockSpec(memory_space=pltpu.VMEM)
    any_spec = pl.BlockSpec(memory_space=pl.ANY)
    dma = pltpu.SemaphoreType.DMA
    stream, queries_keys = pl.pallas_call(
        kernel,
        out_shape=(pltpu.VMEM((width, TOK), BF16), pltpu.VMEM((TOK, heads), BF16)),
        in_specs=[any_spec] * 5,
        out_specs=(vmem_spec, vmem_spec),
        scratch_shapes=[
            pltpu.VMEM((NY, 2 * TOK, depth), BF16),
            pltpu.VMEM((width, depth), BF16),
            pltpu.VMEM((width, TOK), BF16),
            pltpu.VMEM((width,), BF16),
            pltpu.VMEM((COLS, 1, width), F32),
            pltpu.VMEM((NZ, 1, NX * width), F32),
            pltpu.VMEM((NZ, NX * width, heads), BF16),
            pltpu.VMEM((TOK, heads), F32),
            pltpu.VMEM((NY, width, TOK), BF16),
            pltpu.VMEM((NY, width, TOK), BF16),
            pltpu.VMEM((NY - 1, width, TOK), BF16),
            pltpu.VMEM((NY - 1, width, TOK), BF16),
            pltpu.VMEM((COLS, width, TOK), BF16),
            pltpu.VMEM((NZ, 2, TOK), F32),
            pltpu.VMEM((NX, 2, TOK), F32),
            dma((16,)),
            dma((NY,)), dma((NY,)), dma((NY - 1,)), dma((NY - 1,)),
            dma((NX - 1,)), dma((NX,)), dma((NZ - 1,)), dma((NZ,)),
            dma((NX - 1,)), dma((NX,)), dma((NZ - 1,)), dma((NZ,)),
            dma((48,)), dma((48,)),
        ],
        compiler_params=pltpu.CompilerParams(
            collective_id=0, has_side_effects=True, vmem_limit_bytes=56 * 1024 * 1024
        ),
    )(
        hidden, down_weight.T, residual.T, gain,
        qk_weight.reshape(NZ, NX * width, heads),
    )
    stream, queries_keys = pl.pallas_call(
        deliver,
        out_shape=(
            jax.ShapeDtypeStruct((width, TOK), BF16),
            jax.ShapeDtypeStruct((TOK, heads), BF16),
        ),
        in_specs=[vmem_spec] * 2,
        out_specs=(any_spec, any_spec),
        scratch_shapes=[dma((2,))],
    )(
        pltpu.with_memory_space_constraint(stream, pltpu.VMEM),
        pltpu.with_memory_space_constraint(queries_keys, pltpu.VMEM),
    )
    return stream.T, queries_keys


def solution(mesh):
    placed = (P(None, "row"), P("row", "col"), P("row", "col"), P("col"), P(None, "col"))
    return jax.shard_map(
        per_device,
        mesh=mesh,
        in_specs=placed,
        out_specs=(P("row", "col"), P("row", "col")),
        check_vma=False,
    )
```

```python
import functools

import jax
import jax.numpy as jnp
from jax import lax
from jax.experimental import pallas as pl
from jax.experimental.pallas import tpu as pltpu
from jax.sharding import PartitionSpec as P

MESH = pl.DeviceIdType.MESH
F32, BF16 = jnp.float32, jnp.bfloat16
NX, NZ, NY = 4, 8, 4
ROWS, COLS = 2 * NY, NZ * NX
TOK = 128
CUTS = 3
X_FIRST = 48
STEPS_Z = (1, -1, 2, -2, 3, -3, 4)
STEPS_X = (1, -1, 2)

SHARE_AT = 12
MERGE_AT = ("z", -2)
ORDER = (
    ("s", "z", 1), ("s", "z", -1), ("s", "bx", 2), ("s", "x", 0, -1), ("s", "bx", -1), ("s", "z", 2), ("s", "z", 3),
    ("s", "bx", 1), ("s", "z", -3), ("s", "z", -2), ("s", "x", 0, 2), ("s", "x", 0, 1), ("w", "z", 1),
    ("s", "x", 1, 2), ("w", "z", -1), ("s", "x", 1, -1), ("s", "x", 1, 1), ("s", "x", -1, 2), ("s", "x", -1, -1),
    ("w", "bx"), ("s", "bz", -3), ("s", "bz", 3), ("s", "bz", -1), ("s", "x", -1, 1), ("s", "bz", 1), ("w", "z", 2),
    ("s", "x", 2, 2), ("s", "x", 2, 1), ("s", "x", 2, -1), ("w", "z", 3), ("s", "x", 3, 1), ("w", "z", -3),
    ("s", "z4", 3), ("s", "x", -3, -1), ("w", "z", -2), ("s", "z4", -3), ("s", "bz", 2), ("s", "bz", -2),
    ("s", "x", 3, 2), ("s", "x", -2, 1), ("s", "x", -2, -1), ("s", "bz", 4), ("s", "x", -3, 2), ("s", "x", -3, 1),
    ("s", "x", 3, -1), ("s", "x", -2, 2), ("w", "z4"), ("s", "x", 4, 2), ("s", "x", 4, 1),
    ("s", "x", 4, -1), ("c", 0), ("c", 1), ("c", -1), ("c", 3), ("c", -3), ("c", 2), ("c", -2), ("c", 4),
)


def merge(stats, count):
    means, squares = stats[:, 0], stats[:, 1]
    mean = jnp.mean(means, axis=0, keepdims=True)
    off = means - mean
    square = jnp.sum(squares, axis=0, keepdims=True) + count * jnp.sum(off * off, axis=0, keepdims=True)
    return jnp.concatenate([mean, square], axis=0)


def kernel(
    hidden, down, residual, gain, weight, stream_out, qk_out,
    hid_v, down_v, acc, res_v, gain_in, gains, gain_rows, w_v, qk_v,
    pair_send, pair_recv, rs_send, rs_recv, g, stats_z, stats_x,
    load_sem, pair_ssem, pair_rsem, rs_ssem, rs_rsem, gx_ssem, gx_rsem, gz_ssem, gz_rsem,
    sx_ssem, sx_rsem, sz_ssem, sz_rsem,
    ag_ssem, z_rsem, bx_rsem, bz_rsem, x_rsem,
):
    row, col = lax.axis_index("row"), lax.axis_index("col")
    y, core = row // 2, row % 2
    z, x = col // NX, col % NX
    wide = down.shape[0]

    def at(zz, xx):
        return (row, zz * NX + xx)

    def zs(d):
        return lax.rem(z + d + NZ, NZ)

    def xs(d):
        return lax.rem(x + d + NX, NX)

    def load(src, dst, sem):
        copy = pltpu.make_async_copy(src, dst, load_sem.at[sem])
        copy.start()
        return copy

    step = down.shape[1] // CUTS
    c_gain = load(gain, gain_in, 0)
    c_down, c_half = [], ([], [])
    for k in range(CUTS):
        span = slice(k * step, (k + 1) * step)
        c_down.append(load(down.at[:, span], down_v.at[:, span], 4 + k))
        c_half[0].append(load(hidden.at[:, 1 - core, :, span], hid_v.at[0, :, :, span], 4 + CUTS + k))
    for k in range(CUTS):
        span = slice(k * step, (k + 1) * step)
        c_half[1].append(load(hidden.at[:, core, :, span], hid_v.at[1, :, :, span], 4 + 2 * CUTS + k))

    barrier = pltpu.get_barrier_semaphore()
    sibling = (y * 2 + 1 - core, col)
    peers = [sibling] + [(lax.rem(y + d, NY) * 2 + core, col) for d in range(1, NY)]
    peers += [at(z, xs(d)) for d in STEPS_X]
    peers += [at(zs(d), x) for d in STEPS_Z]
    for peer in peers:
        pl.semaphore_signal(barrier, inc=1, device_id=peer, device_id_type=MESH)

    def send(src, dst, ssem, rsem, peer):
        copy = pltpu.make_async_remote_copy(
            src_ref=src, dst_ref=dst, send_sem=ssem, recv_sem=rsem,
            device_id=peer, device_id_type=MESH,
        )
        copy.start()

    def arrived(ref, rsem):
        pltpu.make_async_copy(ref, ref, rsem).wait()

    def over_x(ref, ssem, rsem):
        for d in STEPS_X:
            send(ref, ref, ssem, rsem, at(z, xs(d)))

    def over_z(ref, ssem, rsem):
        for d in STEPS_Z:
            send(ref, ref, ssem, rsem, at(zs(d), x))

    def project(half):
        for k in range(CUTS):
            span = slice(k * step, (k + 1) * step)
            if half == 0:
                c_down[k].wait()
            c_half[half][k].wait()
            tokens = hid_v[half, :, :, span].reshape(NY * TOK, step)
            part = lax.dot_general(
                down_v[:, span], tokens, (((1,), (1,)), ((), ())), preferred_element_type=F32
            )
            if k == 0:
                acc[...] = part
            else:
                acc[...] += part

    project(0)
    for k in range(NY):
        pair_send[k] = acc[:, k * TOK:(k + 1) * TOK].astype(BF16)
    c_gain.wait()
    gains[col] = gain_in[...].astype(F32).reshape(1, wide)
    pl.semaphore_wait(barrier, len(peers))
    send(pair_send, pair_recv, pair_ssem, pair_rsem, sibling)
    over_x(gains.at[col], gx_ssem, gx_rsem)
    c_res = load(residual, res_v, 1)
    project(1)
    arrived(pair_recv, pair_rsem)
    for k in range(NY):
        acc[:, k * TOK:(k + 1) * TOK] += pair_recv[k].astype(F32)
    for d in (2, 1, 3):
        yy = lax.rem(y + d, NY)
        piece = acc[:, pl.ds(pl.multiple_of(yy * TOK, TOK), TOK)]
        rs_send[d - 1] = piece.astype(BF16)
        peer = (yy * 2 + core, col)
        send(rs_send.at[d - 1], rs_recv.at[NY - 1 - d], rs_ssem, rs_rsem, peer)
    own = acc[:, pl.ds(pl.multiple_of(y * TOK, TOK), TOK)]

    c_w = load(weight, w_v, 2)

    arrived(gains.at[pl.ds(0, NX - 1)], gx_rsem)
    over_z(gains.at[pl.ds(z * NX, NX)], gz_ssem, gz_rsem)
    c_res.wait()
    total = res_v[...].astype(F32) + own
    arrived(rs_recv, rs_rsem)
    for d in range(NY - 1):
        total = total + rs_recv[d].astype(F32)
    stream = total.astype(BF16)
    g[col] = stream

    last = pl.ds(X_FIRST, wide - X_FIRST)
    first = pl.ds(0, X_FIRST)
    middle = X_FIRST + 64
    halves = {3: pl.ds(X_FIRST, 64), -3: pl.ds(middle, wide - middle)}

    def place(dz, dx):
        return zs(dz) * NX + xs(dx)

    def group(dz):
        return g.at[pl.ds(zs(dz) * NX, NX), first]

    def sent(kind, step):
        if kind == "z":
            return g.at[col, last], at(zs(step[0]), x)
        if kind == "z4":
            return g.at[place(-step[0], 0), halves[step[0]]], at(zs(step[0] // 3), x)
        if kind == "bx":
            return g.at[col, first], at(z, xs(step[0]))
        if kind == "bz":
            return group(0), at(zs(step[0]), x)
        return g.at[place(-step[0], 0), last], at(z, xs(step[1]))

    z_steps = STEPS_Z[:-1]
    groups = (0,) + STEPS_Z

    def semaphore(kind, step):
        if kind == "z":
            return z_rsem.at[z_steps.index(step[0])]
        if kind == "z4":
            return z_rsem.at[len(z_steps)]
        if kind == "bx":
            return bx_rsem
        if kind == "bz":
            return bz_rsem.at[STEPS_Z.index(step[0])]
        return x_rsem.at[groups.index(step[0])]

    def take(kind, step):
        if kind == "z":
            arrived(g.at[place(-step[0], 0), last], semaphore(kind, step))
        elif kind == "z4":
            arrived(g.at[place(4, 0), last], semaphore(kind, step))
        elif kind == "bx":
            arrived(g.at[pl.ds(z * NX, NX - 1), first], semaphore(kind, step))
        elif kind == "bz":
            arrived(group(-step[0]), semaphore(kind, step))
        else:
            arrived(g.at[pl.ds(zs(-step[0]) * NX, NX - 1), last], semaphore(kind, step))

    computes = [op[1] for op in ORDER if op[0] == "c"]

    def share_statistics():
        values = stream.astype(F32)
        mean = jnp.mean(values, axis=0, keepdims=True)
        off = values - mean
        stats_z[z] = jnp.concatenate([mean, jnp.sum(off * off, axis=0, keepdims=True)], axis=0)
        over_z(stats_z.at[z], sz_ssem, sz_rsem)
        stream_out[...] = stream

    def merge_statistics():
        arrived(stats_z.at[pl.ds(0, NZ - 1)], sz_rsem)
        stats_x[x] = merge(stats_z[...], wide)
        over_x(stats_x.at[x], sx_ssem, sx_rsem)

    def before_compute():
        arrived(gains.at[pl.ds(0, COLS - NX)], gz_rsem)
        for c in range(NZ):
            gain_rows[c] = jnp.concatenate([gains[c * NX + k] for k in range(NX)], axis=1)
        arrived(stats_x.at[pl.ds(0, NX - 1)], sx_rsem)
        both = merge(stats_x[...], NZ * wide)
        scale = 1.0 / jnp.sqrt(both[1:] * (1.0 / (COLS * wide)) + 1e-6)
        mean_t = jnp.transpose(jnp.broadcast_to(both[:1], (TOK, TOK)))
        scale_t = jnp.transpose(jnp.broadcast_to(scale, (TOK, TOK)))
        c_w.wait()
        return mean_t, scale_t

    def project_group(d, mean_t, scale_t):
        zz = zs(-d)
        block = g[pl.ds(zz * NX, NX)].reshape(NX * wide, TOK)
        tokens = jnp.transpose(block)
        row_gain = gain_rows[zz]
        pieces = []
        for k in range(NX * wide // TOK):
            lanes = slice(k * TOK, (k + 1) * TOK)
            piece = (tokens[:, lanes].astype(F32) - mean_t) * scale_t * row_gain[:, lanes]
            pieces.append(piece.astype(BF16))
        out = jnp.dot(jnp.concatenate(pieces, axis=1), w_v[zz], preferred_element_type=F32)
        if d == computes[0]:
            qk_v[...] = out
        elif d != computes[-1]:
            qk_v[...] += out
        else:
            qk_out[...] = (qk_v[...] + out).astype(BF16)

    moments = None
    started = 0
    for op, kind, *step in ORDER:
        if op == "c":
            if moments is None:
                moments = before_compute()
            take("x", (kind,))
            if kind:
                take("bz", (kind,))
            project_group(kind, *moments)
        elif op == "s":
            ref, peer = sent(kind, step)
            send(ref, ref, ag_ssem, semaphore(kind, step), peer)
            started += 1
            if started == SHARE_AT:
                share_statistics()
        else:
            take(kind, step)
            if (kind, *step) == MERGE_AT:
                merge_statistics()

    arrived(pair_send, pair_ssem)
    arrived(rs_send, rs_ssem)
    arrived(gains.at[pl.ds(0, NX - 1)], gx_ssem)
    arrived(gains.at[pl.ds(0, COLS - NX)], gz_ssem)
    arrived(stats_z.at[pl.ds(0, NZ - 1)], sz_ssem)
    arrived(stats_x.at[pl.ds(0, NX - 1)], sx_ssem)
    arrived(g.at[pl.ds(0, COLS - 1)], ag_ssem)


def deliver(stream, queries_keys, stream_out, qk_out, sem):
    copies = [
        pltpu.make_async_copy(stream, stream_out, sem.at[0]),
        pltpu.make_async_copy(queries_keys, qk_out, sem.at[1]),
    ]
    for copy in copies:
        copy.start()
    for copy in copies:
        copy.wait()


def per_device(hidden, down_weight, residual, gain, qk_weight):
    depth, width = down_weight.shape
    full, heads = qk_weight.shape
    vmem_spec = pl.BlockSpec(memory_space=pltpu.VMEM)
    any_spec = pl.BlockSpec(memory_space=pl.ANY)
    dma = pltpu.SemaphoreType.DMA
    stream, queries_keys = pl.pallas_call(
        kernel,
        out_shape=(pltpu.VMEM((width, TOK), BF16), pltpu.VMEM((TOK, heads), BF16)),
        in_specs=[any_spec] * 5,
        out_specs=(vmem_spec, vmem_spec),
        scratch_shapes=[
            pltpu.VMEM((2, NY, TOK, depth), BF16),
            pltpu.VMEM((width, depth), BF16),
            pltpu.VMEM((width, NY * TOK), F32),
            pltpu.VMEM((width, TOK), BF16),
            pltpu.VMEM((width,), BF16),
            pltpu.VMEM((COLS, 1, width), F32),
            pltpu.VMEM((NZ, 1, NX * width), F32),
            pltpu.VMEM((NZ, NX * width, heads), BF16),
            pltpu.VMEM((TOK, heads), F32),
            pltpu.VMEM((NY, width, TOK), BF16),
            pltpu.VMEM((NY, width, TOK), BF16),
            pltpu.VMEM((NY - 1, width, TOK), BF16),
            pltpu.VMEM((NY - 1, width, TOK), BF16),
            pltpu.VMEM((COLS, width, TOK), BF16),
            pltpu.VMEM((NZ, 2, TOK), F32),
            pltpu.VMEM((NX, 2, TOK), F32),
            dma((4 + 3 * CUTS,)),
            *[dma(())] * 12,
            dma(()), dma((NZ - 1,)), dma(()), dma((NZ - 1,)), dma((NZ,)),
        ],
        compiler_params=pltpu.CompilerParams(
            collective_id=0, has_side_effects=True, vmem_limit_bytes=56 * 1024 * 1024
        ),
    )(
        hidden.reshape(NY, 2, TOK, depth), down_weight.T, residual.T, gain,
        qk_weight.reshape(NZ, NX * width, heads),
    )
    stream, queries_keys = pl.pallas_call(
        deliver,
        out_shape=(
            jax.ShapeDtypeStruct((width, TOK), BF16),
            jax.ShapeDtypeStruct((TOK, heads), BF16),
        ),
        in_specs=[vmem_spec] * 2,
        out_specs=(any_spec, any_spec),
        scratch_shapes=[dma((2,))],
    )(
        pltpu.with_memory_space_constraint(stream, pltpu.VMEM),
        pltpu.with_memory_space_constraint(queries_keys, pltpu.VMEM),
    )
    return stream.T, queries_keys


def solution(mesh):
    placed = (P(None, "row"), P("row", "col"), P("row", "col"), P("col"), P(None, "col"))
    return jax.shard_map(
        per_device,
        mesh=mesh,
        in_specs=placed,
        out_specs=(P("row", "col"), P("row", "col")),
        check_vma=False,
    )
```

```python
import functools

import jax
import jax.numpy as jnp
from jax import lax
from jax.experimental import pallas as pl
from jax.experimental.pallas import tpu as pltpu
from jax.sharding import PartitionSpec as P

MESH = pl.DeviceIdType.MESH
F32, BF16 = jnp.float32, jnp.bfloat16
NX, NZ, NY = 4, 8, 4
ROWS, COLS = 2 * NY, NZ * NX
TOK = 128
CUTS = 4
X_FIRST = 48
STEPS_Z = (1, -1, 2, -2, 3, -3, 4)
STEPS_X = (1, -1, 2)

SHARE_AT = 12
MERGE_AT = ("z", -2)
ORDER = (
    ("s", "z", 1), ("s", "z", -1), ("s", "bx", 2), ("s", "x", 0, -1), ("s", "bx", -1), ("s", "z", 2), ("s", "z", 3),
    ("s", "bx", 1), ("s", "z", -3), ("s", "z", -2), ("s", "x", 0, 2), ("s", "x", 0, 1), ("w", "z", 1),
    ("s", "x", 1, 2), ("w", "z", -1), ("s", "x", 1, -1), ("s", "x", 1, 1), ("s", "x", -1, 2), ("s", "x", -1, -1),
    ("w", "bx"), ("s", "bz", -3), ("s", "bz", 3), ("s", "bz", -1), ("s", "x", -1, 1), ("s", "bz", 1), ("w", "z", 2),
    ("s", "x", 2, 2), ("s", "x", 2, 1), ("s", "x", 2, -1), ("w", "z", 3), ("s", "x", 3, 1), ("w", "z", -3),
    ("s", "z4", 3), ("s", "x", -3, -1), ("w", "z", -2), ("s", "z4", -3), ("s", "bz", 2), ("s", "bz", -2),
    ("s", "x", 3, 2), ("s", "x", -2, 1), ("s", "x", -2, -1), ("s", "bz", 4), ("s", "x", -3, 2), ("s", "x", -3, 1),
    ("s", "x", 3, -1), ("s", "x", -2, 2), ("w", "z4"), ("s", "x", 4, 2), ("s", "x", 4, 1),
    ("s", "x", 4, -1), ("c", 0), ("c", 1), ("c", -1), ("c", 3), ("c", -3), ("c", 2), ("c", -2), ("c", 4),
)


def merge(stats, count):
    means, squares = stats[:, 0], stats[:, 1]
    mean = jnp.mean(means, axis=0, keepdims=True)
    off = means - mean
    square = jnp.sum(squares, axis=0, keepdims=True) + count * jnp.sum(off * off, axis=0, keepdims=True)
    return jnp.concatenate([mean, square], axis=0)


def kernel(
    hidden, down, residual, gain, weight, stream_out, qk_out,
    hid_v, down_v, acc, res_v, gain_in, gains, gain_rows, w_v, qk_v,
    pair_send, pair_recv, rs_send, rs_recv, g, stats_z, stats_x,
    load_sem, pair_ssem, pair_rsem, rs_ssem, rs_rsem, gx_ssem, gx_rsem, gz_ssem, gz_rsem,
    sx_ssem, sx_rsem, sz_ssem, sz_rsem,
    ag_ssem, z_rsem, bx_rsem, bz_rsem, x_rsem,
):
    row, col = lax.axis_index("row"), lax.axis_index("col")
    y, core = row // 2, row % 2
    z, x = col // NX, col % NX
    wide = down.shape[0]

    def at(zz, xx):
        return (row, zz * NX + xx)

    def zs(d):
        return lax.rem(z + d + NZ, NZ)

    def xs(d):
        return lax.rem(x + d + NX, NX)

    def load(src, dst, sem):
        copy = pltpu.make_async_copy(src, dst, load_sem.at[sem])
        copy.start()
        return copy

    step = down.shape[1] // CUTS
    c_gain = load(gain, gain_in, 0)
    c_down, c_half = [], ([], [])
    for k in range(CUTS):
        span = slice(k * step, (k + 1) * step)
        c_down.append(load(down.at[:, span], down_v.at[:, span], 4 + k))
        c_half[0].append(load(hidden.at[:, 1 - core, :, span], hid_v.at[0, :, :, span], 4 + CUTS + k))
    for k in range(CUTS):
        span = slice(k * step, (k + 1) * step)
        c_half[1].append(load(hidden.at[:, core, :, span], hid_v.at[1, :, :, span], 4 + 2 * CUTS + k))

    barrier = pltpu.get_barrier_semaphore()
    sibling = (y * 2 + 1 - core, col)
    peers = [sibling] + [(lax.rem(y + d, NY) * 2 + core, col) for d in range(1, NY)]
    peers += [at(z, xs(d)) for d in STEPS_X]
    peers += [at(zs(d), x) for d in STEPS_Z]
    for peer in peers:
        pl.semaphore_signal(barrier, inc=1, device_id=peer, device_id_type=MESH)

    def send(src, dst, ssem, rsem, peer):
        copy = pltpu.make_async_remote_copy(
            src_ref=src, dst_ref=dst, send_sem=ssem, recv_sem=rsem,
            device_id=peer, device_id_type=MESH,
        )
        copy.start()

    def arrived(ref, rsem):
        pltpu.make_async_copy(ref, ref, rsem).wait()

    def over_x(ref, ssem, rsem):
        for d in STEPS_X:
            send(ref, ref, ssem, rsem, at(z, xs(d)))

    def over_z(ref, ssem, rsem):
        for d in STEPS_Z:
            send(ref, ref, ssem, rsem, at(zs(d), x))

    def project(half):
        for k in range(CUTS):
            span = slice(k * step, (k + 1) * step)
            if half == 0:
                c_down[k].wait()
            c_half[half][k].wait()
            tokens = hid_v[half, :, :, span].reshape(NY * TOK, step)
            part = lax.dot_general(
                down_v[:, span], tokens, (((1,), (1,)), ((), ())), preferred_element_type=F32
            )
            if k == 0:
                acc[...] = part
            else:
                acc[...] += part

    project(0)
    for k in range(NY):
        pair_send[k] = acc[:, k * TOK:(k + 1) * TOK].astype(BF16)
    c_gain.wait()
    gains[col] = gain_in[...].astype(F32).reshape(1, wide)
    pl.semaphore_wait(barrier, len(peers))
    send(pair_send, pair_recv, pair_ssem, pair_rsem, sibling)
    over_x(gains.at[col], gx_ssem, gx_rsem)
    c_res = load(residual, res_v, 1)
    project(1)
    arrived(pair_recv, pair_rsem)
    for k in range(NY):
        acc[:, k * TOK:(k + 1) * TOK] += pair_recv[k].astype(F32)
    for d in (2, 1, 3):
        yy = lax.rem(y + d, NY)
        piece = acc[:, pl.ds(pl.multiple_of(yy * TOK, TOK), TOK)]
        rs_send[d - 1] = piece.astype(BF16)
        peer = (yy * 2 + core, col)
        send(rs_send.at[d - 1], rs_recv.at[NY - 1 - d], rs_ssem, rs_rsem, peer)
    own = acc[:, pl.ds(pl.multiple_of(y * TOK, TOK), TOK)]

    c_w = load(weight, w_v, 2)

    arrived(gains.at[pl.ds(0, NX - 1)], gx_rsem)
    over_z(gains.at[pl.ds(z * NX, NX)], gz_ssem, gz_rsem)
    c_res.wait()
    total = res_v[...].astype(F32) + own
    arrived(rs_recv, rs_rsem)
    for d in range(NY - 1):
        total = total + rs_recv[d].astype(F32)
    stream = total.astype(BF16)
    g[col] = stream

    last = pl.ds(X_FIRST, wide - X_FIRST)
    first = pl.ds(0, X_FIRST)
    middle = X_FIRST + 64
    halves = {3: pl.ds(X_FIRST, 64), -3: pl.ds(middle, wide - middle)}

    def place(dz, dx):
        return zs(dz) * NX + xs(dx)

    def group(dz):
        return g.at[pl.ds(zs(dz) * NX, NX), first]

    def sent(kind, step):
        if kind == "z":
            return g.at[col, last], at(zs(step[0]), x)
        if kind == "z4":
            return g.at[place(-step[0], 0), halves[step[0]]], at(zs(step[0] // 3), x)
        if kind == "bx":
            return g.at[col, first], at(z, xs(step[0]))
        if kind == "bz":
            return group(0), at(zs(step[0]), x)
        return g.at[place(-step[0], 0), last], at(z, xs(step[1]))

    z_steps = STEPS_Z[:-1]
    groups = (0,) + STEPS_Z

    def semaphore(kind, step):
        if kind == "z":
            return z_rsem.at[z_steps.index(step[0])]
        if kind == "z4":
            return z_rsem.at[len(z_steps)]
        if kind == "bx":
            return bx_rsem
        if kind == "bz":
            return bz_rsem.at[STEPS_Z.index(step[0])]
        return x_rsem.at[groups.index(step[0])]

    def take(kind, step):
        if kind == "z":
            arrived(g.at[place(-step[0], 0), last], semaphore(kind, step))
        elif kind == "z4":
            arrived(g.at[place(4, 0), last], semaphore(kind, step))
        elif kind == "bx":
            arrived(g.at[pl.ds(z * NX, NX - 1), first], semaphore(kind, step))
        elif kind == "bz":
            arrived(group(-step[0]), semaphore(kind, step))
        else:
            arrived(g.at[pl.ds(zs(-step[0]) * NX, NX - 1), last], semaphore(kind, step))

    computes = [op[1] for op in ORDER if op[0] == "c"]

    def share_statistics():
        values = stream.astype(F32)
        mean = jnp.mean(values, axis=0, keepdims=True)
        off = values - mean
        stats_z[z] = jnp.concatenate([mean, jnp.sum(off * off, axis=0, keepdims=True)], axis=0)
        over_z(stats_z.at[z], sz_ssem, sz_rsem)
        stream_out[...] = stream
        arrived(gains.at[pl.ds(0, COLS - NX)], gz_rsem)
        for c in range(NZ):
            gain_rows[c] = jnp.concatenate([gains[c * NX + k] for k in range(NX)], axis=1)

    def merge_statistics():
        arrived(stats_z.at[pl.ds(0, NZ - 1)], sz_rsem)
        stats_x[x] = merge(stats_z[...], wide)
        over_x(stats_x.at[x], sx_ssem, sx_rsem)

    def before_compute():
        arrived(stats_x.at[pl.ds(0, NX - 1)], sx_rsem)
        both = merge(stats_x[...], NZ * wide)
        scale = 1.0 / jnp.sqrt(both[1:] * (1.0 / (COLS * wide)) + 1e-6)
        mean_t = jnp.transpose(jnp.broadcast_to(both[:1], (TOK, TOK)))
        scale_t = jnp.transpose(jnp.broadcast_to(scale, (TOK, TOK)))
        c_w.wait()
        return mean_t, scale_t

    def project_group(d, mean_t, scale_t):
        zz = zs(-d)
        block = g[pl.ds(zz * NX, NX)].reshape(NX * wide, TOK)
        tokens = jnp.transpose(block)
        row_gain = gain_rows[zz]
        pieces = []
        for k in range(NX * wide // TOK):
            lanes = slice(k * TOK, (k + 1) * TOK)
            piece = (tokens[:, lanes].astype(F32) - mean_t) * scale_t * row_gain[:, lanes]
            pieces.append(piece.astype(BF16))
        out = jnp.dot(jnp.concatenate(pieces, axis=1), w_v[zz], preferred_element_type=F32)
        if d == computes[0]:
            qk_v[...] = out
        elif d != computes[-1]:
            qk_v[...] += out
        else:
            qk_out[...] = (qk_v[...] + out).astype(BF16)

    moments = None
    started = 0
    for op, kind, *step in ORDER:
        if op == "c":
            if moments is None:
                moments = before_compute()
            take("x", (kind,))
            if kind:
                take("bz", (kind,))
            project_group(kind, *moments)
        elif op == "s":
            ref, peer = sent(kind, step)
            send(ref, ref, ag_ssem, semaphore(kind, step), peer)
            started += 1
            if started == SHARE_AT:
                share_statistics()
        else:
            take(kind, step)
            if (kind, *step) == MERGE_AT:
                merge_statistics()

    arrived(pair_send, pair_ssem)
    arrived(rs_send, rs_ssem)
    arrived(gains.at[pl.ds(0, NX - 1)], gx_ssem)
    arrived(gains.at[pl.ds(0, COLS - NX)], gz_ssem)
    arrived(stats_z.at[pl.ds(0, NZ - 1)], sz_ssem)
    arrived(stats_x.at[pl.ds(0, NX - 1)], sx_ssem)
    arrived(g.at[pl.ds(0, COLS - 1)], ag_ssem)


def deliver(stream, queries_keys, stream_out, qk_out, sem):
    copies = [
        pltpu.make_async_copy(stream, stream_out, sem.at[0]),
        pltpu.make_async_copy(queries_keys, qk_out, sem.at[1]),
    ]
    for copy in copies:
        copy.start()
    for copy in copies:
        copy.wait()


def per_device(hidden, down_weight, residual, gain, qk_weight):
    depth, width = down_weight.shape
    full, heads = qk_weight.shape
    vmem_spec = pl.BlockSpec(memory_space=pltpu.VMEM)
    any_spec = pl.BlockSpec(memory_space=pl.ANY)
    dma = pltpu.SemaphoreType.DMA
    stream, queries_keys = pl.pallas_call(
        kernel,
        out_shape=(pltpu.VMEM((width, TOK), BF16), pltpu.VMEM((TOK, heads), BF16)),
        in_specs=[any_spec] * 5,
        out_specs=(vmem_spec, vmem_spec),
        scratch_shapes=[
            pltpu.VMEM((2, NY, TOK, depth), BF16),
            pltpu.VMEM((width, depth), BF16),
            pltpu.VMEM((width, NY * TOK), F32),
            pltpu.VMEM((width, TOK), BF16),
            pltpu.VMEM((width,), BF16),
            pltpu.VMEM((COLS, 1, width), F32),
            pltpu.VMEM((NZ, 1, NX * width), F32),
            pltpu.VMEM((NZ, NX * width, heads), BF16),
            pltpu.VMEM((TOK, heads), F32),
            pltpu.VMEM((NY, width, TOK), BF16),
            pltpu.VMEM((NY, width, TOK), BF16),
            pltpu.VMEM((NY - 1, width, TOK), BF16),
            pltpu.VMEM((NY - 1, width, TOK), BF16),
            pltpu.VMEM((COLS, width, TOK), BF16),
            pltpu.VMEM((NZ, 2, TOK), F32),
            pltpu.VMEM((NX, 2, TOK), F32),
            dma((4 + 3 * CUTS,)),
            *[dma(())] * 12,
            dma(()), dma((NZ - 1,)), dma(()), dma((NZ - 1,)), dma((NZ,)),
        ],
        compiler_params=pltpu.CompilerParams(
            collective_id=0, has_side_effects=True, vmem_limit_bytes=56 * 1024 * 1024
        ),
    )(
        hidden.reshape(NY, 2, TOK, depth), down_weight.T, residual.T, gain,
        qk_weight.reshape(NZ, NX * width, heads),
    )
    stream, queries_keys = pl.pallas_call(
        deliver,
        out_shape=(
            jax.ShapeDtypeStruct((width, TOK), BF16),
            jax.ShapeDtypeStruct((TOK, heads), BF16),
        ),
        in_specs=[vmem_spec] * 2,
        out_specs=(any_spec, any_spec),
        scratch_shapes=[dma((2,))],
    )(
        pltpu.with_memory_space_constraint(stream, pltpu.VMEM),
        pltpu.with_memory_space_constraint(queries_keys, pltpu.VMEM),
    )
    return stream.T, queries_keys


def solution(mesh):
    placed = (P(None, "row"), P("row", "col"), P("row", "col"), P("col"), P(None, "col"))
    return jax.shard_map(
        per_device,
        mesh=mesh,
        in_specs=placed,
        out_specs=(P("row", "col"), P("row", "col")),
        check_vma=False,
    )
```

```python
import functools

import jax
import jax.numpy as jnp
from jax import lax
from jax.experimental import pallas as pl
from jax.experimental.pallas import tpu as pltpu
from jax.sharding import PartitionSpec as P

MESH = pl.DeviceIdType.MESH
F32, BF16 = jnp.float32, jnp.bfloat16
NX, NZ, NY = 4, 8, 4
ROWS, COLS = 2 * NY, NZ * NX
TOK = 128
CUTS = 4
X_FIRST = 48
STEPS_Z = (1, -1, 2, -2, 3, -3, 4)
STEPS_X = (1, -1, 2)

SHARE_AT = 12
MERGE_AT = ("z", -2)
ORDER = (
    ("s", "z", 1), ("s", "z", -1), ("s", "bx", 2), ("s", "x", 0, -1), ("s", "bx", -1), ("s", "z", 2), ("s", "z", 3),
    ("s", "bx", 1), ("s", "z", -3), ("s", "z", -2), ("s", "x", 0, 2), ("s", "x", 0, 1), ("w", "z", 1),
    ("s", "x", 1, 2), ("w", "z", -1), ("s", "x", 1, -1), ("s", "x", 1, 1), ("s", "x", -1, 2), ("s", "x", -1, -1),
    ("w", "bx"), ("s", "bz", -3), ("s", "bz", 3), ("s", "bz", -1), ("s", "x", -1, 1), ("s", "bz", 1), ("w", "z", 2),
    ("s", "x", 2, 2), ("s", "x", 2, 1), ("s", "x", 2, -1), ("w", "z", 3), ("s", "x", 3, 1), ("w", "z", -3),
    ("s", "z4", 3), ("s", "x", -3, -1), ("w", "z", -2), ("s", "z4", -3), ("s", "bz", 2), ("s", "bz", -2),
    ("s", "x", 3, 2), ("s", "x", -2, 1), ("s", "x", -2, -1), ("s", "bz", 4), ("s", "x", -3, 2), ("s", "x", -3, 1),
    ("s", "x", 3, -1), ("s", "x", -2, 2), ("w", "z4"), ("s", "x", 4, 2), ("s", "x", 4, 1),
    ("s", "x", 4, -1), ("c", 0), ("c", 1), ("c", -1), ("c", 3), ("c", -3), ("c", 2), ("c", -2), ("c", 4),
)


def merge(stats, count):
    means, squares = stats[:, 0], stats[:, 1]
    mean = jnp.mean(means, axis=0, keepdims=True)
    off = means - mean
    square = jnp.sum(squares, axis=0, keepdims=True) + count * jnp.sum(off * off, axis=0, keepdims=True)
    return jnp.concatenate([mean, square], axis=0)


def kernel(
    hidden, down, residual, gain, weight, stream_out, qk_out,
    hid_v, down_v, acc, res_v, gain_in, gains, gain_rows, w_v, qk_v,
    pair_send, pair_recv, rs_send, rs_recv, g, stats_z, stats_x,
    load_sem, pair_ssem, pair_rsem, rs_ssem, rs_rsem, gx_ssem, gx_rsem, gz_ssem, gz_rsem,
    sx_ssem, sx_rsem, sz_ssem, sz_rsem,
    ag_ssem, z_rsem, bx_rsem, bz_rsem, x_rsem,
):
    row, col = lax.axis_index("row"), lax.axis_index("col")
    y, core = row // 2, row % 2
    z, x = col // NX, col % NX
    wide = down.shape[0]

    def at(zz, xx):
        return (row, zz * NX + xx)

    def zs(d):
        return lax.rem(z + d + NZ, NZ)

    def xs(d):
        return lax.rem(x + d + NX, NX)

    def load(src, dst, sem):
        copy = pltpu.make_async_copy(src, dst, load_sem.at[sem])
        copy.start()
        return copy

    barrier = pltpu.get_barrier_semaphore()
    sibling = (y * 2 + 1 - core, col)
    peers = [sibling] + [(lax.rem(y + d, NY) * 2 + core, col) for d in range(1, NY)]
    peers += [at(z, xs(d)) for d in STEPS_X]
    peers += [at(zs(d), x) for d in STEPS_Z]
    for peer in peers:
        pl.semaphore_signal(barrier, inc=1, device_id=peer, device_id_type=MESH)

    step = down.shape[1] // CUTS
    c_gain = load(gain, gain_in, 0)
    c_down, c_half = [], ([], [])
    for k in range(CUTS):
        span = slice(k * step, (k + 1) * step)
        c_down.append(load(down.at[:, span], down_v.at[:, span], 4 + k))
        c_half[0].append(load(hidden.at[:, 1 - core, :, span], hid_v.at[0, :, :, span], 4 + CUTS + k))
    for k in range(CUTS):
        span = slice(k * step, (k + 1) * step)
        c_half[1].append(load(hidden.at[:, core, :, span], hid_v.at[1, :, :, span], 4 + 2 * CUTS + k))

    def send(src, dst, ssem, rsem, peer):
        copy = pltpu.make_async_remote_copy(
            src_ref=src, dst_ref=dst, send_sem=ssem, recv_sem=rsem,
            device_id=peer, device_id_type=MESH,
        )
        copy.start()

    def arrived(ref, rsem):
        pltpu.make_async_copy(ref, ref, rsem).wait()

    def over_x(ref, ssem, rsem):
        for d in STEPS_X:
            send(ref, ref, ssem, rsem, at(z, xs(d)))

    def over_z(ref, ssem, rsem):
        for d in STEPS_Z:
            send(ref, ref, ssem, rsem, at(zs(d), x))

    def project(half):
        for k in range(CUTS):
            span = slice(k * step, (k + 1) * step)
            if half == 0:
                c_down[k].wait()
            c_half[half][k].wait()
            tokens = hid_v[half, :, :, span].reshape(NY * TOK, step)
            part = lax.dot_general(
                down_v[:, span], tokens, (((1,), (1,)), ((), ())), preferred_element_type=F32
            )
            if k == 0:
                acc[...] = part
            else:
                acc[...] += part

    project(0)
    for k in range(NY):
        pair_send[k] = acc[:, k * TOK:(k + 1) * TOK].astype(BF16)
    c_gain.wait()
    gains[col] = gain_in[...].astype(F32).reshape(1, wide)
    pl.semaphore_wait(barrier, len(peers))
    send(pair_send, pair_recv, pair_ssem, pair_rsem, sibling)
    over_x(gains.at[col], gx_ssem, gx_rsem)
    c_res = load(residual, res_v, 1)
    project(1)
    arrived(pair_recv, pair_rsem)

    def summed(place):
        return acc[:, pl.ds(pl.multiple_of(place * TOK, TOK), TOK)] + pair_recv[place].astype(F32)

    for d in (2, 1, 3):
        yy = lax.rem(y + d, NY)
        piece = summed(yy)
        rs_send[d - 1] = piece.astype(BF16)
        peer = (yy * 2 + core, col)
        send(rs_send.at[d - 1], rs_recv.at[NY - 1 - d], rs_ssem, rs_rsem, peer)
    own = summed(y)

    c_w = load(weight, w_v, 2)

    arrived(gains.at[pl.ds(0, NX - 1)], gx_rsem)
    over_z(gains.at[pl.ds(z * NX, NX)], gz_ssem, gz_rsem)
    c_res.wait()
    total = res_v[...].astype(F32) + own
    arrived(rs_recv, rs_rsem)
    for d in range(NY - 1):
        total = total + rs_recv[d].astype(F32)
    stream = total.astype(BF16)
    g[col] = stream

    last = pl.ds(X_FIRST, wide - X_FIRST)
    first = pl.ds(0, X_FIRST)
    middle = X_FIRST + 64
    halves = {3: pl.ds(X_FIRST, 64), -3: pl.ds(middle, wide - middle)}

    def place(dz, dx):
        return zs(dz) * NX + xs(dx)

    def group(dz):
        return g.at[pl.ds(zs(dz) * NX, NX), first]

    def sent(kind, step):
        if kind == "z":
            return g.at[col, last], at(zs(step[0]), x)
        if kind == "z4":
            return g.at[place(-step[0], 0), halves[step[0]]], at(zs(step[0] // 3), x)
        if kind == "bx":
            return g.at[col, first], at(z, xs(step[0]))
        if kind == "bz":
            return group(0), at(zs(step[0]), x)
        return g.at[place(-step[0], 0), last], at(z, xs(step[1]))

    z_steps = STEPS_Z[:-1]
    groups = (0,) + STEPS_Z

    def semaphore(kind, step):
        if kind == "z":
            return z_rsem.at[z_steps.index(step[0])]
        if kind == "z4":
            return z_rsem.at[len(z_steps)]
        if kind == "bx":
            return bx_rsem
        if kind == "bz":
            return bz_rsem.at[STEPS_Z.index(step[0])]
        return x_rsem.at[groups.index(step[0])]

    def take(kind, step):
        if kind == "z":
            arrived(g.at[place(-step[0], 0), last], semaphore(kind, step))
        elif kind == "z4":
            arrived(g.at[place(4, 0), last], semaphore(kind, step))
        elif kind == "bx":
            arrived(g.at[pl.ds(z * NX, NX - 1), first], semaphore(kind, step))
        elif kind == "bz":
            arrived(group(-step[0]), semaphore(kind, step))
        else:
            arrived(g.at[pl.ds(zs(-step[0]) * NX, NX - 1), last], semaphore(kind, step))

    computes = [op[1] for op in ORDER if op[0] == "c"]

    def share_statistics():
        values = stream.astype(F32)
        mean = jnp.mean(values, axis=0, keepdims=True)
        off = values - mean
        stats_z[z] = jnp.concatenate([mean, jnp.sum(off * off, axis=0, keepdims=True)], axis=0)
        over_z(stats_z.at[z], sz_ssem, sz_rsem)
        stream_out[...] = stream
        arrived(gains.at[pl.ds(0, COLS - NX)], gz_rsem)
        for c in range(NZ):
            gain_rows[c] = jnp.concatenate([gains[c * NX + k] for k in range(NX)], axis=1)

    def merge_statistics():
        arrived(stats_z.at[pl.ds(0, NZ - 1)], sz_rsem)
        stats_x[x] = merge(stats_z[...], wide)
        over_x(stats_x.at[x], sx_ssem, sx_rsem)

    def before_compute():
        arrived(stats_x.at[pl.ds(0, NX - 1)], sx_rsem)
        both = merge(stats_x[...], NZ * wide)
        scale = 1.0 / jnp.sqrt(both[1:] * (1.0 / (COLS * wide)) + 1e-6)
        mean_t = jnp.transpose(jnp.broadcast_to(both[:1], (TOK, TOK)))
        scale_t = jnp.transpose(jnp.broadcast_to(scale, (TOK, TOK)))
        c_w.wait()
        return mean_t, scale_t

    def project_group(d, mean_t, scale_t):
        zz = zs(-d)
        block = g[pl.ds(zz * NX, NX)].reshape(NX * wide, TOK)
        tokens = jnp.transpose(block)
        row_gain = gain_rows[zz]
        pieces = []
        for k in range(NX * wide // TOK):
            lanes = slice(k * TOK, (k + 1) * TOK)
            piece = (tokens[:, lanes].astype(F32) - mean_t) * scale_t * row_gain[:, lanes]
            pieces.append(piece.astype(BF16))
        out = jnp.dot(jnp.concatenate(pieces, axis=1), w_v[zz], preferred_element_type=F32)
        if d == computes[0]:
            qk_v[...] = out
        elif d != computes[-1]:
            qk_v[...] += out
        else:
            qk_out[...] = (qk_v[...] + out).astype(BF16)

    moments = None
    started = 0
    for op, kind, *step in ORDER:
        if op == "c":
            if moments is None:
                moments = before_compute()
            take("x", (kind,))
            if kind:
                take("bz", (kind,))
            project_group(kind, *moments)
        elif op == "s":
            ref, peer = sent(kind, step)
            send(ref, ref, ag_ssem, semaphore(kind, step), peer)
            started += 1
            if started == SHARE_AT:
                share_statistics()
        else:
            take(kind, step)
            if (kind, *step) == MERGE_AT:
                merge_statistics()

    arrived(pair_send, pair_ssem)
    arrived(rs_send, rs_ssem)
    arrived(gains.at[pl.ds(0, NX - 1)], gx_ssem)
    arrived(gains.at[pl.ds(0, COLS - NX)], gz_ssem)
    arrived(stats_z.at[pl.ds(0, NZ - 1)], sz_ssem)
    arrived(stats_x.at[pl.ds(0, NX - 1)], sx_ssem)
    arrived(g.at[pl.ds(0, COLS - 1)], ag_ssem)


def deliver(stream, queries_keys, stream_out, qk_out, sem):
    copies = [
        pltpu.make_async_copy(stream, stream_out, sem.at[0]),
        pltpu.make_async_copy(queries_keys, qk_out, sem.at[1]),
    ]
    for copy in copies:
        copy.start()
    for copy in copies:
        copy.wait()


def per_device(hidden, down_weight, residual, gain, qk_weight):
    depth, width = down_weight.shape
    full, heads = qk_weight.shape
    vmem_spec = pl.BlockSpec(memory_space=pltpu.VMEM)
    any_spec = pl.BlockSpec(memory_space=pl.ANY)
    dma = pltpu.SemaphoreType.DMA
    stream, queries_keys = pl.pallas_call(
        kernel,
        out_shape=(pltpu.VMEM((width, TOK), BF16), pltpu.VMEM((TOK, heads), BF16)),
        in_specs=[any_spec] * 5,
        out_specs=(vmem_spec, vmem_spec),
        scratch_shapes=[
            pltpu.VMEM((2, NY, TOK, depth), BF16),
            pltpu.VMEM((width, depth), BF16),
            pltpu.VMEM((width, NY * TOK), F32),
            pltpu.VMEM((width, TOK), BF16),
            pltpu.VMEM((width,), BF16),
            pltpu.VMEM((COLS, 1, width), F32),
            pltpu.VMEM((NZ, 1, NX * width), F32),
            pltpu.VMEM((NZ, NX * width, heads), BF16),
            pltpu.VMEM((TOK, heads), F32),
            pltpu.VMEM((NY, width, TOK), BF16),
            pltpu.VMEM((NY, width, TOK), BF16),
            pltpu.VMEM((NY - 1, width, TOK), BF16),
            pltpu.VMEM((NY - 1, width, TOK), BF16),
            pltpu.VMEM((COLS, width, TOK), BF16),
            pltpu.VMEM((NZ, 2, TOK), F32),
            pltpu.VMEM((NX, 2, TOK), F32),
            dma((4 + 3 * CUTS,)),
            *[dma(())] * 12,
            dma(()), dma((NZ - 1,)), dma(()), dma((NZ - 1,)), dma((NZ,)),
        ],
        compiler_params=pltpu.CompilerParams(
            collective_id=0, has_side_effects=True, vmem_limit_bytes=56 * 1024 * 1024
        ),
    )(
        hidden.reshape(NY, 2, TOK, depth), down_weight.T, residual.T, gain,
        qk_weight.reshape(NZ, NX * width, heads),
    )
    stream, queries_keys = pl.pallas_call(
        deliver,
        out_shape=(
            jax.ShapeDtypeStruct((width, TOK), BF16),
            jax.ShapeDtypeStruct((TOK, heads), BF16),
        ),
        in_specs=[vmem_spec] * 2,
        out_specs=(any_spec, any_spec),
        scratch_shapes=[dma((2,))],
    )(
        pltpu.with_memory_space_constraint(stream, pltpu.VMEM),
        pltpu.with_memory_space_constraint(queries_keys, pltpu.VMEM),
    )
    return stream.T, queries_keys


def solution(mesh):
    placed = (P(None, "row"), P("row", "col"), P("row", "col"), P("col"), P(None, "col"))
    return jax.shard_map(
        per_device,
        mesh=mesh,
        in_specs=placed,
        out_specs=(P("row", "col"), P("row", "col")),
        check_vma=False,
    )
```

```python
import functools

import jax
import jax.numpy as jnp
from jax import lax
from jax.experimental import pallas as pl
from jax.experimental.pallas import tpu as pltpu
from jax.sharding import PartitionSpec as P

MESH = pl.DeviceIdType.MESH
F32, BF16 = jnp.float32, jnp.bfloat16
NX, NZ, NY = 4, 8, 4
ROWS, COLS = 2 * NY, NZ * NX
TOK = 128
CUTS = 4
X_FIRST = 48
STEPS_Z = (1, -1, 2, -2, 3, -3, 4)
STEPS_X = (1, -1, 2)

SHARE_AT = 12
MERGE_AT = ("z", -2)
ORDER = (
    ("s", "z", 1), ("s", "z", -1), ("s", "bx", 2), ("s", "x", 0, -1), ("s", "bx", -1), ("s", "z", 2), ("s", "z", 3),
    ("s", "bx", 1), ("s", "z", -3), ("s", "z", -2), ("s", "x", 0, 2), ("s", "x", 0, 1), ("w", "z", 1),
    ("s", "x", 1, 2), ("w", "z", -1), ("s", "x", 1, -1), ("s", "x", 1, 1), ("s", "x", -1, 2), ("s", "x", -1, -1),
    ("w", "bx"), ("s", "bz", -3), ("s", "bz", 3), ("s", "bz", -1), ("s", "x", -1, 1), ("s", "bz", 1), ("w", "z", 2),
    ("s", "x", 2, 2), ("s", "x", 2, 1), ("s", "x", 2, -1), ("w", "z", 3), ("s", "x", 3, 1), ("w", "z", -3),
    ("s", "z4", 3), ("s", "x", -3, -1), ("w", "z", -2), ("s", "z4", -3), ("s", "bz", 2), ("s", "bz", -2),
    ("s", "x", 3, 2), ("s", "x", -2, 1), ("s", "x", -2, -1), ("s", "bz", 4), ("s", "x", -3, 2), ("s", "x", -3, 1),
    ("s", "x", 3, -1), ("s", "x", -2, 2), ("w", "z4"), ("s", "x", 4, 2), ("s", "x", 4, 1),
    ("s", "x", 4, -1), ("c", 0), ("c", 1), ("c", -1), ("c", 3), ("c", -3), ("c", 2), ("c", -2), ("c", 4),
)


def merge(stats, count):
    means, squares = stats[:, 0], stats[:, 1]
    mean = jnp.mean(means, axis=0, keepdims=True)
    off = means - mean
    square = jnp.sum(squares, axis=0, keepdims=True) + count * jnp.sum(off * off, axis=0, keepdims=True)
    return jnp.concatenate([mean, square], axis=0)


def kernel(
    hidden, down, residual, gain, weight, stream_out, qk_out,
    hid_v, down_v, acc, res_v, gain_in, gains, gain_rows, w_v, qk_v,
    pair_send, pair_recv, rs_send, rs_recv, g, stats_z, stats_x,
    load_sem, pair_ssem, pair_rsem, rs_ssem, rs_rsem, gx_ssem, gx_rsem, gz_ssem, gz_rsem,
    sx_ssem, sx_rsem, sz_ssem, sz_rsem,
    ag_ssem, z_rsem, bx_rsem, bz_rsem, x_rsem,
):
    row, col = lax.axis_index("row"), lax.axis_index("col")
    y, core = row // 2, row % 2
    z, x = col // NX, col % NX
    wide = down.shape[0]

    def at(zz, xx):
        return (row, zz * NX + xx)

    def zs(d):
        return lax.rem(z + d + NZ, NZ)

    def xs(d):
        return lax.rem(x + d + NX, NX)

    def load(src, dst, sem):
        copy = pltpu.make_async_copy(src, dst, load_sem.at[sem])
        copy.start()
        return copy

    step = down.shape[1] // CUTS
    c_gain = load(gain, gain_in, 0)
    c_down, c_half = [], ([], [])
    for k in range(CUTS):
        span = slice(k * step, (k + 1) * step)
        c_down.append(load(down.at[:, span], down_v.at[:, span], 4 + k))
        c_half[0].append(load(hidden.at[:, 1 - core, :, span], hid_v.at[0, :, :, span], 4 + CUTS + k))
    for k in range(CUTS):
        span = slice(k * step, (k + 1) * step)
        c_half[1].append(load(hidden.at[:, core, :, span], hid_v.at[1, :, :, span], 4 + 2 * CUTS + k))

    barrier = pltpu.get_barrier_semaphore()
    sibling = (y * 2 + 1 - core, col)
    peers = [sibling] + [(lax.rem(y + d, NY) * 2 + core, col) for d in range(1, NY)]
    peers += [at(z, xs(d)) for d in STEPS_X]
    peers += [at(zs(d), x) for d in STEPS_Z]
    for peer in peers:
        pl.semaphore_signal(barrier, inc=1, device_id=peer, device_id_type=MESH)

    def send(src, dst, ssem, rsem, peer):
        copy = pltpu.make_async_remote_copy(
            src_ref=src, dst_ref=dst, send_sem=ssem, recv_sem=rsem,
            device_id=peer, device_id_type=MESH,
        )
        copy.start()

    def arrived(ref, rsem):
        pltpu.make_async_copy(ref, ref, rsem).wait()

    def over_x(ref, ssem, rsem):
        for d in STEPS_X:
            send(ref, ref, ssem, rsem, at(z, xs(d)))

    def over_z(ref, ssem, rsem):
        for d in STEPS_Z:
            send(ref, ref, ssem, rsem, at(zs(d), x))

    def project(half):
        for k in range(CUTS):
            span = slice(k * step, (k + 1) * step)
            if half == 0:
                c_down[k].wait()
            c_half[half][k].wait()
            tokens = hid_v[half, :, :, span].reshape(NY * TOK, step)
            part = lax.dot_general(
                down_v[:, span], tokens, (((1,), (1,)), ((), ())), preferred_element_type=F32
            )
            if k == 0:
                acc[...] = part
            else:
                acc[...] += part

    project(0)
    for k in range(NY):
        pair_send[k] = acc[:, k * TOK:(k + 1) * TOK].astype(BF16)
    c_gain.wait()
    gains[col] = gain_in[...].astype(F32).reshape(1, wide)
    pl.semaphore_wait(barrier, len(peers))
    send(pair_send, pair_recv, pair_ssem, pair_rsem, sibling)
    over_x(gains.at[col], gx_ssem, gx_rsem)
    c_res = load(residual, res_v, 1)
    project(1)
    arrived(pair_recv, pair_rsem)

    def summed(place):
        return acc[:, pl.ds(pl.multiple_of(place * TOK, TOK), TOK)] + pair_recv[place].astype(F32)

    for d in (2, 1, 3):
        yy = lax.rem(y + d, NY)
        piece = summed(yy)
        rs_send[d - 1] = piece.astype(BF16)
        peer = (yy * 2 + core, col)
        send(rs_send.at[d - 1], rs_recv.at[NY - 1 - d], rs_ssem, rs_rsem, peer)
    own = summed(y)

    arrived(gains.at[pl.ds(0, NX - 1)], gx_rsem)
    over_z(gains.at[pl.ds(z * NX, NX)], gz_ssem, gz_rsem)
    c_res.wait()
    total = res_v[...].astype(F32) + own
    arrived(rs_recv, rs_rsem)
    for d in range(NY - 1):
        total = total + rs_recv[d].astype(F32)
    stream = total.astype(BF16)
    g[col] = stream

    last = pl.ds(X_FIRST, wide - X_FIRST)
    first = pl.ds(0, X_FIRST)
    middle = X_FIRST + 64
    halves = {3: pl.ds(X_FIRST, 64), -3: pl.ds(middle, wide - middle)}

    def place(dz, dx):
        return zs(dz) * NX + xs(dx)

    def group(dz):
        return g.at[pl.ds(zs(dz) * NX, NX), first]

    def sent(kind, step):
        if kind == "z":
            return g.at[col, last], at(zs(step[0]), x)
        if kind == "z4":
            return g.at[place(-step[0], 0), halves[step[0]]], at(zs(step[0] // 3), x)
        if kind == "bx":
            return g.at[col, first], at(z, xs(step[0]))
        if kind == "bz":
            return group(0), at(zs(step[0]), x)
        return g.at[place(-step[0], 0), last], at(z, xs(step[1]))

    z_steps = STEPS_Z[:-1]
    groups = (0,) + STEPS_Z

    def semaphore(kind, step):
        if kind == "z":
            return z_rsem.at[z_steps.index(step[0])]
        if kind == "z4":
            return z_rsem.at[len(z_steps)]
        if kind == "bx":
            return bx_rsem
        if kind == "bz":
            return bz_rsem.at[STEPS_Z.index(step[0])]
        return x_rsem.at[groups.index(step[0])]

    def take(kind, step):
        if kind == "z":
            arrived(g.at[place(-step[0], 0), last], semaphore(kind, step))
        elif kind == "z4":
            arrived(g.at[place(4, 0), last], semaphore(kind, step))
        elif kind == "bx":
            arrived(g.at[pl.ds(z * NX, NX - 1), first], semaphore(kind, step))
        elif kind == "bz":
            arrived(group(-step[0]), semaphore(kind, step))
        else:
            arrived(g.at[pl.ds(zs(-step[0]) * NX, NX - 1), last], semaphore(kind, step))

    computes = [op[1] for op in ORDER if op[0] == "c"]

    def share_statistics():
        values = stream.astype(F32)
        mean = jnp.mean(values, axis=0, keepdims=True)
        off = values - mean
        stats_z[z] = jnp.concatenate([mean, jnp.sum(off * off, axis=0, keepdims=True)], axis=0)
        over_z(stats_z.at[z], sz_ssem, sz_rsem)
        stream_out[...] = stream
        arrived(gains.at[pl.ds(0, COLS - NX)], gz_rsem)
        for c in range(NZ):
            gain_rows[c] = jnp.concatenate([gains[c * NX + k] for k in range(NX)], axis=1)

    def merge_statistics():
        arrived(stats_z.at[pl.ds(0, NZ - 1)], sz_rsem)
        stats_x[x] = merge(stats_z[...], wide)
        over_x(stats_x.at[x], sx_ssem, sx_rsem)

    def before_compute():
        arrived(stats_x.at[pl.ds(0, NX - 1)], sx_rsem)
        both = merge(stats_x[...], NZ * wide)
        scale = 1.0 / jnp.sqrt(both[1:] * (1.0 / (COLS * wide)) + 1e-6)
        mean_t = jnp.transpose(jnp.broadcast_to(both[:1], (TOK, TOK)))
        scale_t = jnp.transpose(jnp.broadcast_to(scale, (TOK, TOK)))
        c_w.wait()
        return mean_t, scale_t

    def project_group(d, mean_t, scale_t):
        zz = zs(-d)
        block = g[pl.ds(zz * NX, NX)].reshape(NX * wide, TOK)
        tokens = jnp.transpose(block)
        row_gain = gain_rows[zz]
        pieces = []
        for k in range(NX * wide // TOK):
            lanes = slice(k * TOK, (k + 1) * TOK)
            piece = (tokens[:, lanes].astype(F32) - mean_t) * scale_t * row_gain[:, lanes]
            pieces.append(piece.astype(BF16))
        out = jnp.dot(jnp.concatenate(pieces, axis=1), w_v[zz], preferred_element_type=F32)
        if d == computes[0]:
            qk_v[...] = out
        elif d != computes[-1]:
            qk_v[...] += out
        else:
            qk_out[...] = (qk_v[...] + out).astype(BF16)

    moments = None
    c_w = load(weight, w_v, 2)
    started = 0
    for op, kind, *step in ORDER:
        if op == "c":
            if moments is None:
                moments = before_compute()
            take("x", (kind,))
            if kind:
                take("bz", (kind,))
            project_group(kind, *moments)
        elif op == "s":
            ref, peer = sent(kind, step)
            send(ref, ref, ag_ssem, semaphore(kind, step), peer)
            started += 1
            if started == SHARE_AT:
                share_statistics()
        else:
            take(kind, step)
            if (kind, *step) == MERGE_AT:
                merge_statistics()

    arrived(pair_send, pair_ssem)
    arrived(rs_send, rs_ssem)
    arrived(gains.at[pl.ds(0, NX - 1)], gx_ssem)
    arrived(gains.at[pl.ds(0, COLS - NX)], gz_ssem)
    arrived(stats_z.at[pl.ds(0, NZ - 1)], sz_ssem)
    arrived(stats_x.at[pl.ds(0, NX - 1)], sx_ssem)
    arrived(g.at[pl.ds(0, COLS - 1)], ag_ssem)


def deliver(stream, queries_keys, stream_out, qk_out, sem):
    copies = [
        pltpu.make_async_copy(stream, stream_out, sem.at[0]),
        pltpu.make_async_copy(queries_keys, qk_out, sem.at[1]),
    ]
    for copy in copies:
        copy.start()
    for copy in copies:
        copy.wait()


def per_device(hidden, down_weight, residual, gain, qk_weight):
    depth, width = down_weight.shape
    full, heads = qk_weight.shape
    vmem_spec = pl.BlockSpec(memory_space=pltpu.VMEM)
    any_spec = pl.BlockSpec(memory_space=pl.ANY)
    dma = pltpu.SemaphoreType.DMA
    stream, queries_keys = pl.pallas_call(
        kernel,
        out_shape=(pltpu.VMEM((width, TOK), BF16), pltpu.VMEM((TOK, heads), BF16)),
        in_specs=[any_spec] * 5,
        out_specs=(vmem_spec, vmem_spec),
        scratch_shapes=[
            pltpu.VMEM((2, NY, TOK, depth), BF16),
            pltpu.VMEM((width, depth), BF16),
            pltpu.VMEM((width, NY * TOK), F32),
            pltpu.VMEM((width, TOK), BF16),
            pltpu.VMEM((width,), BF16),
            pltpu.VMEM((COLS, 1, width), F32),
            pltpu.VMEM((NZ, 1, NX * width), F32),
            pltpu.VMEM((NZ, NX * width, heads), BF16),
            pltpu.VMEM((TOK, heads), F32),
            pltpu.VMEM((NY, width, TOK), BF16),
            pltpu.VMEM((NY, width, TOK), BF16),
            pltpu.VMEM((NY - 1, width, TOK), BF16),
            pltpu.VMEM((NY - 1, width, TOK), BF16),
            pltpu.VMEM((COLS, width, TOK), BF16),
            pltpu.VMEM((NZ, 2, TOK), F32),
            pltpu.VMEM((NX, 2, TOK), F32),
            dma((4 + 3 * CUTS,)),
            *[dma(())] * 12,
            dma(()), dma((NZ - 1,)), dma(()), dma((NZ - 1,)), dma((NZ,)),
        ],
        compiler_params=pltpu.CompilerParams(
            collective_id=0, has_side_effects=True, vmem_limit_bytes=56 * 1024 * 1024
        ),
    )(
        hidden.reshape(NY, 2, TOK, depth), down_weight.T, residual.T, gain,
        qk_weight.reshape(NZ, NX * width, heads),
    )
    stream, queries_keys = pl.pallas_call(
        deliver,
        out_shape=(
            jax.ShapeDtypeStruct((width, TOK), BF16),
            jax.ShapeDtypeStruct((TOK, heads), BF16),
        ),
        in_specs=[vmem_spec] * 2,
        out_specs=(any_spec, any_spec),
        scratch_shapes=[dma((2,))],
    )(
        pltpu.with_memory_space_constraint(stream, pltpu.VMEM),
        pltpu.with_memory_space_constraint(queries_keys, pltpu.VMEM),
    )
    return stream.T, queries_keys


def solution(mesh):
    placed = (P(None, "row"), P("row", "col"), P("row", "col"), P("col"), P(None, "col"))
    return jax.shard_map(
        per_device,
        mesh=mesh,
        in_specs=placed,
        out_specs=(P("row", "col"), P("row", "col")),
        check_vma=False,
    )
```

```python
import functools

import jax
import jax.numpy as jnp
from jax import lax
from jax.experimental import pallas as pl
from jax.experimental.pallas import tpu as pltpu
from jax.sharding import PartitionSpec as P

MESH = pl.DeviceIdType.MESH
F32, BF16 = jnp.float32, jnp.bfloat16
NX, NZ, NY = 4, 8, 4
ROWS, COLS = 2 * NY, NZ * NX
TOK = 128
CUTS = 4
X_FIRST = 48
STEPS_Z = (1, -1, 2, -2, 3, -3, 4)
STEPS_X = (1, -1, 2)

SHARE_AT = 12
MERGE_AT = ("z", -2)
ORDER = (
    ("s", "z", 1), ("s", "z", -1), ("s", "bx", 2), ("s", "x", 0, -1), ("s", "bx", -1), ("s", "z", 2), ("s", "z", 3),
    ("s", "bx", 1), ("s", "z", -3), ("s", "z", -2), ("s", "x", 0, 2), ("s", "x", 0, 1), ("w", "z", 1),
    ("s", "x", 1, 2), ("w", "z", -1), ("s", "x", 1, -1), ("s", "x", 1, 1), ("s", "x", -1, 2), ("s", "x", -1, -1),
    ("w", "bx"), ("s", "bz", -3), ("s", "bz", 3), ("s", "bz", -1), ("s", "x", -1, 1), ("s", "bz", 1), ("w", "z", 2),
    ("s", "x", 2, 2), ("s", "x", 2, 1), ("s", "x", 2, -1), ("w", "z", 3), ("s", "x", 3, 1), ("w", "z", -3),
    ("s", "z4", 3), ("s", "x", -3, -1), ("w", "z", -2), ("s", "z4", -3), ("s", "bz", 2), ("s", "bz", -2),
    ("s", "x", 3, 2), ("s", "x", -2, 1), ("s", "x", -2, -1), ("s", "bz", 4), ("s", "x", -3, 2), ("s", "x", -3, 1),
    ("s", "x", 3, -1), ("s", "x", -2, 2), ("w", "z4"), ("s", "x", 4, 2), ("s", "x", 4, 1),
    ("s", "x", 4, -1), ("c", 0), ("c", 1), ("c", -1), ("c", 3), ("c", -3), ("c", 2), ("c", -2), ("c", 4),
)


def merge(stats, count):
    means, squares = stats[:, 0], stats[:, 1]
    mean = jnp.mean(means, axis=0, keepdims=True)
    off = means - mean
    square = jnp.sum(squares, axis=0, keepdims=True) + count * jnp.sum(off * off, axis=0, keepdims=True)
    return jnp.concatenate([mean, square], axis=0)


def kernel(
    hidden, down, residual, gain, weight, stream_out, qk_out,
    hid_v, down_v, acc, res_v, gain_in, gains, gain_rows, w_v, qk_v,
    pair_send, pair_recv, rs_send, rs_recv, g, stats_z, stats_x,
    load_sem, pair_ssem, pair_rsem, rs_ssem, rs_rsem, gx_ssem, gx_rsem, gz_ssem, gz_rsem,
    sx_ssem, sx_rsem, sz_ssem, sz_rsem,
    ag_ssem, z_rsem, bx_rsem, bz_rsem, x_rsem,
):
    row, col = lax.axis_index("row"), lax.axis_index("col")
    y, core = row // 2, row % 2
    z, x = col // NX, col % NX
    wide = down.shape[0]

    def at(zz, xx):
        return (row, zz * NX + xx)

    def zs(d):
        return lax.rem(z + d + NZ, NZ)

    def xs(d):
        return lax.rem(x + d + NX, NX)

    def load(src, dst, sem):
        copy = pltpu.make_async_copy(src, dst, load_sem.at[sem])
        copy.start()
        return copy

    step = down.shape[1] // CUTS
    c_gain = load(gain, gain_in, 0)
    c_down, c_half = [], ([], [])
    for k in range(CUTS):
        span = slice(k * step, (k + 1) * step)
        c_down.append(load(down.at[:, span], down_v.at[:, span], 4 + k))
        c_half[0].append(load(hidden.at[:, 1 - core, :, span], hid_v.at[0, :, :, span], 4 + CUTS + k))
    for k in range(CUTS):
        span = slice(k * step, (k + 1) * step)
        c_half[1].append(load(hidden.at[:, core, :, span], hid_v.at[1, :, :, span], 4 + 2 * CUTS + k))

    barrier = pltpu.get_barrier_semaphore()
    sibling = (y * 2 + 1 - core, col)
    peers = [sibling] + [(lax.rem(y + d, NY) * 2 + core, col) for d in range(1, NY)]
    peers += [at(z, xs(d)) for d in STEPS_X]
    peers += [at(zs(d), x) for d in STEPS_Z]
    for peer in peers:
        pl.semaphore_signal(barrier, inc=1, device_id=peer, device_id_type=MESH)

    def send(src, dst, ssem, rsem, peer):
        copy = pltpu.make_async_remote_copy(
            src_ref=src, dst_ref=dst, send_sem=ssem, recv_sem=rsem,
            device_id=peer, device_id_type=MESH,
        )
        copy.start()

    def arrived(ref, rsem):
        pltpu.make_async_copy(ref, ref, rsem).wait()

    def over_x(ref, ssem, rsem):
        for d in STEPS_X:
            send(ref, ref, ssem, rsem, at(z, xs(d)))

    def over_z(ref, ssem, rsem):
        for d in STEPS_Z:
            send(ref, ref, ssem, rsem, at(zs(d), x))

    def project(half):
        for k in range(CUTS):
            span = slice(k * step, (k + 1) * step)
            if half == 0:
                c_down[k].wait()
            c_half[half][k].wait()
            tokens = hid_v[half, :, :, span].reshape(NY * TOK, step)
            part = lax.dot_general(
                down_v[:, span], tokens, (((1,), (1,)), ((), ())), preferred_element_type=F32
            )
            if k == 0:
                acc[...] = part
            else:
                acc[...] += part

    project(0)
    for k in range(NY):
        pair_send[k] = acc[:, k * TOK:(k + 1) * TOK].astype(BF16)
    c_gain.wait()
    gains[col] = gain_in[...].astype(F32).reshape(1, wide)
    pl.semaphore_wait(barrier, len(peers))
    send(pair_send, pair_recv, pair_ssem, pair_rsem, sibling)
    over_x(gains.at[col], gx_ssem, gx_rsem)
    c_res = load(residual, res_v, 1)
    project(1)
    arrived(pair_recv, pair_rsem)

    def summed(place):
        return acc[:, pl.ds(pl.multiple_of(place * TOK, TOK), TOK)] + pair_recv[place].astype(F32)

    for d in (2, 1, 3):
        yy = lax.rem(y + d, NY)
        piece = summed(yy)
        rs_send[d - 1] = piece.astype(BF16)
        peer = (yy * 2 + core, col)
        send(rs_send.at[d - 1], rs_recv.at[NY - 1 - d], rs_ssem, rs_rsem, peer)
    own = summed(y)

    c_w = load(weight, w_v, 2)

    arrived(gains.at[pl.ds(0, NX - 1)], gx_rsem)
    over_z(gains.at[pl.ds(z * NX, NX)], gz_ssem, gz_rsem)
    c_res.wait()
    total = res_v[...].astype(F32) + own
    arrived(rs_recv, rs_rsem)
    for d in range(NY - 1):
        total = total + rs_recv[d].astype(F32)
    stream = total.astype(BF16)
    g[col] = stream

    last = pl.ds(X_FIRST, wide - X_FIRST)
    first = pl.ds(0, X_FIRST)
    middle = X_FIRST + 64
    halves = {3: pl.ds(X_FIRST, 64), -3: pl.ds(middle, wide - middle)}

    def place(dz, dx):
        return zs(dz) * NX + xs(dx)

    def group(dz):
        return g.at[pl.ds(zs(dz) * NX, NX), first]

    def sent(kind, step):
        if kind == "z":
            return g.at[col, last], at(zs(step[0]), x)
        if kind == "z4":
            return g.at[place(-step[0], 0), halves[step[0]]], at(zs(step[0] // 3), x)
        if kind == "bx":
            return g.at[col, first], at(z, xs(step[0]))
        if kind == "bz":
            return group(0), at(zs(step[0]), x)
        return g.at[place(-step[0], 0), last], at(z, xs(step[1]))

    z_steps = STEPS_Z[:-1]
    groups = (0,) + STEPS_Z

    def semaphore(kind, step):
        if kind == "z":
            return z_rsem.at[z_steps.index(step[0])]
        if kind == "z4":
            return z_rsem.at[len(z_steps)]
        if kind == "bx":
            return bx_rsem
        if kind == "bz":
            return bz_rsem.at[STEPS_Z.index(step[0])]
        return x_rsem.at[groups.index(step[0])]

    def take(kind, step):
        if kind == "z":
            arrived(g.at[place(-step[0], 0), last], semaphore(kind, step))
        elif kind == "z4":
            arrived(g.at[place(4, 0), last], semaphore(kind, step))
        elif kind == "bx":
            arrived(g.at[pl.ds(z * NX, NX - 1), first], semaphore(kind, step))
        elif kind == "bz":
            arrived(group(-step[0]), semaphore(kind, step))
        else:
            arrived(g.at[pl.ds(zs(-step[0]) * NX, NX - 1), last], semaphore(kind, step))

    computes = [op[1] for op in ORDER if op[0] == "c"]

    def share_statistics():
        values = stream.astype(F32)
        mean = jnp.mean(values, axis=0, keepdims=True)
        off = values - mean
        stats_z[z] = jnp.concatenate([mean, jnp.sum(off * off, axis=0, keepdims=True)], axis=0)
        over_z(stats_z.at[z], sz_ssem, sz_rsem)
        stream_out[...] = stream
        arrived(gains.at[pl.ds(0, COLS - NX)], gz_rsem)
        for c in range(NZ):
            gain_rows[c] = jnp.concatenate([gains[c * NX + k] for k in range(NX)], axis=1)

    def merge_statistics():
        arrived(stats_z.at[pl.ds(0, NZ - 1)], sz_rsem)
        stats_x[x] = merge(stats_z[...], wide)
        over_x(stats_x.at[x], sx_ssem, sx_rsem)

    def before_compute():
        arrived(stats_x.at[pl.ds(0, NX - 1)], sx_rsem)
        both = merge(stats_x[...], NZ * wide)
        scale = 1.0 / jnp.sqrt(both[1:] * (1.0 / (COLS * wide)) + 1e-6)
        mean_t = jnp.transpose(jnp.broadcast_to(both[:1], (TOK, TOK)))
        scale_t = jnp.transpose(jnp.broadcast_to(scale, (TOK, TOK)))
        c_w.wait()
        return mean_t, scale_t

    def project_group(d, mean_t, scale_t):
        zz = zs(-d)
        block = g[pl.ds(zz * NX, NX)].reshape(NX * wide, TOK)
        tokens = jnp.transpose(block)
        row_gain = gain_rows[zz]
        pieces = []
        for k in range(NX * wide // TOK):
            lanes = slice(k * TOK, (k + 1) * TOK)
            piece = (tokens[:, lanes].astype(F32) - mean_t) * scale_t * row_gain[:, lanes]
            pieces.append(piece.astype(BF16))
        out = jnp.dot(jnp.concatenate(pieces, axis=1), w_v[zz], preferred_element_type=F32)
        if d == computes[0]:
            qk_v[...] = out
        elif d != computes[-1]:
            qk_v[...] += out
        else:
            qk_out[...] = (qk_v[...] + out).astype(BF16)

    moments = None
    started = 0
    for op, kind, *step in ORDER:
        if op == "c":
            if moments is None:
                moments = before_compute()
            take("x", (kind,))
            if kind:
                take("bz", (kind,))
            project_group(kind, *moments)
        elif op == "s":
            ref, peer = sent(kind, step)
            send(ref, ref, ag_ssem, semaphore(kind, step), peer)
            started += 1
            if started == SHARE_AT:
                share_statistics()
        else:
            take(kind, step)
            if (kind, *step) == MERGE_AT:
                merge_statistics()

    arrived(pair_send, pair_ssem)
    arrived(rs_send, rs_ssem)
    arrived(gains.at[pl.ds(0, NX - 1)], gx_ssem)
    arrived(gains.at[pl.ds(0, COLS - NX)], gz_ssem)
    arrived(stats_z.at[pl.ds(0, NZ - 1)], sz_ssem)
    arrived(stats_x.at[pl.ds(0, NX - 1)], sx_ssem)
    arrived(g.at[pl.ds(0, COLS - 1)], ag_ssem)


def deliver(stream, queries_keys, stream_out, qk_out, sem):
    copies = [
        pltpu.make_async_copy(stream, stream_out, sem.at[0]),
        pltpu.make_async_copy(queries_keys, qk_out, sem.at[1]),
    ]
    for copy in copies:
        copy.start()
    for copy in copies:
        copy.wait()


def per_device(hidden, down_weight, residual, gain, qk_weight):
    depth, width = down_weight.shape
    full, heads = qk_weight.shape
    vmem_spec = pl.BlockSpec(memory_space=pltpu.VMEM)
    any_spec = pl.BlockSpec(memory_space=pl.ANY)
    dma = pltpu.SemaphoreType.DMA
    stream, queries_keys = pl.pallas_call(
        kernel,
        out_shape=(pltpu.VMEM((width, TOK), BF16), pltpu.VMEM((TOK, heads), BF16)),
        in_specs=[any_spec] * 5,
        out_specs=(vmem_spec, vmem_spec),
        scratch_shapes=[
            pltpu.VMEM((2, NY, TOK, depth), BF16),
            pltpu.VMEM((width, depth), BF16),
            pltpu.VMEM((width, NY * TOK), F32),
            pltpu.VMEM((width, TOK), BF16),
            pltpu.VMEM((width,), BF16),
            pltpu.VMEM((COLS, 1, width), F32),
            pltpu.VMEM((NZ, 1, NX * width), F32),
            pltpu.VMEM((NZ, NX * width, heads), BF16),
            pltpu.VMEM((TOK, heads), F32),
            pltpu.VMEM((NY, width, TOK), BF16),
            pltpu.VMEM((NY, width, TOK), BF16),
            pltpu.VMEM((NY - 1, width, TOK), BF16),
            pltpu.VMEM((NY - 1, width, TOK), BF16),
            pltpu.VMEM((COLS, width, TOK), BF16),
            pltpu.VMEM((NZ, 2, TOK), F32),
            pltpu.VMEM((NX, 2, TOK), F32),
            dma((4 + 3 * CUTS,)),
            *[dma(())] * 12,
            dma(()), dma((NZ - 1,)), dma(()), dma((NZ - 1,)), dma((NZ,)),
        ],
        compiler_params=pltpu.CompilerParams(
            collective_id=0, has_side_effects=True, vmem_limit_bytes=56 * 1024 * 1024
        ),
    )(
        hidden.reshape(NY, 2, TOK, depth), down_weight.T, residual.T, gain,
        qk_weight.reshape(NZ, NX * width, heads),
    )
    stream, queries_keys = pl.pallas_call(
        deliver,
        out_shape=(
            jax.ShapeDtypeStruct((width, TOK), BF16),
            jax.ShapeDtypeStruct((TOK, heads), BF16),
        ),
        in_specs=[vmem_spec] * 2,
        out_specs=(any_spec, any_spec),
        scratch_shapes=[dma((2,))],
    )(
        pltpu.with_memory_space_constraint(stream, pltpu.VMEM),
        pltpu.with_memory_space_constraint(queries_keys, pltpu.VMEM),
    )
    return stream.T, queries_keys


def solution(mesh):
    placed = (P(None, "row"), P("row", "col"), P("row", "col"), P("col"), P(None, "col"))
    return jax.shard_map(
        per_device,
        mesh=mesh,
        in_specs=placed,
        out_specs=(P("row", "col"), P("row", "col")),
        check_vma=False,
    )
```
